32 devices in a mesh: wide: 4 (over z), narrow: 8 (over y, x, core).
Axes of the slice: x: 2, y: 2, z: 4, core: 2. Of those that a mesh axis runs over, the one named last changes fastest.
Arguments:
- phase_ids: int32 [512, 512, 256], P('wide', 'narrow'), may hold values from 0 to 3
- conduct_table: float32 [4, 3], replicated, may hold values from 0.2 to 5
- gradient: float32 [3], replicated, may hold values from -3 to 3
- start_field: float32 [512, 512, 256], P('wide', 'narrow'), may hold values from -32 to 32
Outputs:
- solution: float32 [512, 512, 256], P('wide', 'narrow')
- residual_next: float32 [512, 512, 256], P('wide', 'narrow')
- new_direction: float32 [512, 512, 256], P('wide', 'narrow')
The draws below stay inside these ranges and needn't reach their ends.
Inputs may be any that keep to these rules, and one draw needn't show every extreme that they name: `phase_ids`: each voxel's phase indexes a row of conduct_table.
All inputs are finite; a program needn't handle non-finite values.
Results may differ from the reference program's by a relative error of at most 0.0065.
Values sent between devices are 32-bit elements; how exact they have to be, the bound alone decides.
No kernel may reach another device: no remote copies, remote signals or barrier semaphores. Data moves between devices by JAX's collectives and lax.ppermute only.
A program may use at most 256 MiB of HBM per device.

```python
import math
import jax
import jax.numpy as jnp
from jax import lax

NX = 512
NY = 512
NZ = 256
PHASES = 4


def draw_start_field(key, part):
    position = jnp.arange(NX, dtype=jnp.float32) / jnp.float32(max(NX - 1, 1))
    envelope = jnp.exp(position * jnp.log(jnp.float32(4.0)))
    noise = jnp.clip(jax.random.normal(key, (NX, NY, NZ), jnp.float32), -4.0, 4.0)
    return (noise * envelope[:, None, None]).astype(jnp.float32)


def place_ends(values, key, low, top_value):
    longest = values.shape.index(max(values.shape))
    spots = []
    for shift in (0, 1):
        where = [jax.random.randint(jax.random.fold_in(key, axis), (), 0, length) for axis, length in enumerate(values.shape)]
        where[longest] = (where[longest] + shift) % values.shape[longest]
        spots.append(tuple(where))
    return values.at[spots[0]].set(low).at[spots[1]].set(top_value)


def gaussian(own_key, shape, width, limit, held_as=jnp.bfloat16):
    return jnp.clip(width * jax.random.normal(own_key, shape, jnp.float32), -limit, limit).astype(held_as)


def setup_inputs(seed: int = 0) -> dict:
    key_list = jax.random.split(jax.random.key(seed), 5)
    return {
        "phase_ids": place_ends(jax.random.randint(key_list[0], (NX, NY, NZ), 0, PHASES), jax.random.fold_in(key_list[0], 1), 0, PHASES - 1).astype(jnp.int32),
        "conduct_table": jnp.clip(jnp.exp(jax.random.uniform(key_list[1], (PHASES, 3), jnp.float32, math.log(0.2), math.log(5.0))), 0.2, 5.0),
        "gradient": gaussian(key_list[2], (3,), 1.0, 3.0, jnp.float32),
        "start_field": draw_start_field(jax.random.fold_in(key_list[4], 71), 0),
    }


HIGHEST = lax.Precision.HIGHEST
FORWARD_FORMS = ('nyz,mn->myz', 'xnz,mn->xmz', 'xyn,mn->xym')
INVERSE_FORMS = ('myz,mn->nyz', 'xmz,mn->xnz', 'xym,mn->xyn')

def cosine_table(length):
    freq_index = jnp.arange(length, dtype=jnp.int32)[:, None]
    cell_index = jnp.arange(length, dtype=jnp.int32)[None, :]
    wrapped = freq_index * (2 * cell_index + 1) % (4 * length)
    angle_rad = wrapped.astype(jnp.float32) * (jnp.pi / (2.0 * length))
    weight = jnp.where(freq_index == 0, jnp.sqrt(jnp.float32(1.0 / length)), jnp.sqrt(jnp.float32(2.0 / length)))
    return weight.astype(jnp.float32) * jnp.cos(angle_rad)

def eigen_values(length, index):
    angle_rad = index.astype(jnp.float32) * (jnp.pi / length)
    return 2.0 - 2.0 * jnp.cos(angle_rad)

def green_block(base_cond, index_x, index_y, index_z):
    lowest = eigen_values(NX, jnp.ones((), jnp.int32))
    eigen_sum = lowest + eigen_values(NX, index_x)[:, None, None]
    eigen_sum = eigen_sum + eigen_values(NY, index_y)[None, :, None]
    eigen_sum = eigen_sum + eigen_values(NZ, index_z)[None, None, :]
    zero_mode = (index_x[:, None, None] == 0) & (index_y[None, :, None] == 0) & (index_z[None, None, :] == 0)
    return jnp.where(zero_mode, jnp.float32(0.0), 1.0 / (base_cond * eigen_sum))

def transform(values, matrix, axis_dim, inverse):
    einsum_form = INVERSE_FORMS[axis_dim] if inverse else FORWARD_FORMS[axis_dim]
    return jnp.einsum(einsum_form, values, matrix, precision=HIGHEST)

def harmonic(lower_side, upper_side):
    return 2.0 * lower_side * upper_side / (lower_side + upper_side)

def conductivities(phase_ids, conduct_table):
    result = []
    for component in range(3):
        summed = jnp.zeros(phase_ids.shape, jnp.float32)
        for member in range(PHASES):
            summed = summed + jnp.where(phase_ids == member, conduct_table[member, component], jnp.float32(0.0))
        result.append(summed)
    return result

def pad_along(values, axis_dim):
    widths = [(0, 0), (0, 0), (0, 0)]
    widths[axis_dim] = (1, 1)
    return jnp.pad(values, widths)

def face_values(cond_field, axis_dim):
    padded = pad_along(cond_field, axis_dim)
    count = padded.shape[axis_dim]
    lower_side = lax.slice_in_dim(padded, 0, count - 1, axis=axis_dim)
    upper_side = lax.slice_in_dim(padded, 1, count, axis=axis_dim)
    return harmonic(lower_side, upper_side)

def apply_operator(grid_field, faces):
    divergence = None
    for axis_dim in range(3):
        padded = pad_along(grid_field, axis_dim)
        count = padded.shape[axis_dim]
        jump = lax.slice_in_dim(padded, 1, count, axis=axis_dim) - lax.slice_in_dim(padded, 0, count - 1, axis=axis_dim)
        flux = faces[axis_dim] * jump
        part = lax.slice_in_dim(flux, 1, count - 1, axis=axis_dim) - lax.slice_in_dim(flux, 0, count - 2, axis=axis_dim)
        divergence = part if divergence is None else divergence + part
    return -divergence

def precondition(grid_field, tables, green):
    spectral = transform(grid_field, tables[2], 2, False)
    spectral = transform(spectral, tables[1], 1, False)
    spectral = transform(spectral, tables[0], 0, False)
    spectral = spectral * green
    spectral = transform(spectral, tables[0], 0, True)
    spectral = transform(spectral, tables[1], 1, True)
    return transform(spectral, tables[2], 2, True)

def reference(phase_ids, conduct_table, gradient, start_field):
    conds = conductivities(phase_ids, conduct_table)
    faces = [face_values(conds[axis_dim], axis_dim) for axis_dim in range(3)]
    source = gradient[0] * (faces[0][1:] - faces[0][:-1])
    source = source + gradient[1] * (faces[1][:, 1:] - faces[1][:, :-1])
    source = source + gradient[2] * (faces[2][:, :, 1:] - faces[2][:, :, :-1])
    residual = source - apply_operator(start_field, faces)
    tables = (cosine_table(NX), cosine_table(NY), cosine_table(NZ))
    base_cond = jnp.mean(conduct_table)
    green = green_block(base_cond, jnp.arange(NX, dtype=jnp.int32), jnp.arange(NY, dtype=jnp.int32), jnp.arange(NZ, dtype=jnp.int32))
    direction = precondition(residual, tables, green)
    rz_now = jnp.sum(residual * direction)
    image_field = apply_operator(direction, faces)
    curvature = jnp.sum(direction * image_field)
    step_alpha = rz_now / curvature
    solution = start_field + step_alpha * direction
    residual_next = residual - step_alpha * image_field
    preconditioned = precondition(residual_next, tables, green)
    rz_next = jnp.sum(residual_next * preconditioned)
    new_direction = preconditioned + rz_next / rz_now * direction
    return (solution, residual_next, new_direction)
```

```python
import functools

import jax
import jax.numpy as jnp
import ml_dtypes
import numpy as np
from jax import lax
from jax.experimental import pallas as pl
from jax.experimental.pallas import tpu as pltpu
from jax.sharding import PartitionSpec as P

PHASES = 4
F32 = jnp.float32
BF16 = jnp.bfloat16
VMEM_LIMIT = 56 * 1024 * 1024
FORWARD_TERMS = ((0, 0), (0, 1), (1, 0), (1, 1), (0, 2), (2, 0))
INVERSE_TERMS = ((0, 0), (0, 1), (1, 0))


def cosine_table(length):
    m = np.arange(length)[:, None]
    n = np.arange(length)[None, :]
    weight = np.where(m == 0, np.sqrt(1.0 / length), np.sqrt(2.0 / length))
    return weight * np.cos(np.pi * (m * (2 * n + 1) % (4 * length)) / (2.0 * length))


def eigen_values(length):
    return 4.0 * np.sin(np.pi * np.arange(length) / (2.0 * length)) ** 2


def pieces(matrix, count=3):
    rest = np.asarray(matrix, np.float64)
    result = []
    for _ in range(count):
        piece = rest.astype(np.float32).astype(ml_dtypes.bfloat16)
        result.append(piece)
        rest = rest - piece.astype(np.float64)
    return np.stack(result)


def make_tables(size_x, size_y, size_z, wide, narrow):
    length_x = size_x * wide
    group = min(max(256 // size_y, 1), size_x)
    parity = np.concatenate([np.arange(0, size_y, 2), np.arange(1, size_y, 2)])
    strip = cosine_table(size_y)[parity]
    block_y = np.kron(np.eye(group), strip)
    table_z = cosine_table(size_z)
    shift = 4.0 * np.sin(np.pi / (2.0 * length_x)) ** 2
    eig_z = eigen_values(size_z)
    sigma = shift + eigen_values(size_y)[parity][:, None] + eig_z[None, :]
    theta = 2.0 * np.arcsinh(np.sqrt(sigma) / 2.0)
    decay = np.exp(-theta)
    kappa = 1.0 / (2.0 * np.sinh(theta))
    step = np.exp(-theta * size_x)
    total = -np.expm1(-2.0 * wide * size_x * theta)
    powers = np.stack([step**t / total for t in range(2 * wide)])
    border = np.broadcast_to(strip[:, :1], sigma.shape)
    eta = 2.0 * np.arcsinh(
        np.sqrt(shift + eig_z[:, None] + eigen_values(length_x)[None, :]) / 2.0
    )
    fade = np.exp(-eta * size_y)
    half_angle = np.pi * np.arange(1, narrow) / (2.0 * narrow)
    capacity = (np.tanh(eta / 2.0) * -np.expm1(-2.0 * eta * size_y))[None] / (
        (np.expm1(-eta * size_y) ** 2)[None]
        + 4.0 * fade[None] * (np.sin(half_angle) ** 2)[:, None, None]
    )
    part_z = size_z // narrow
    capacity = capacity.reshape(narrow - 1, narrow, part_z, length_x).transpose(1, 0, 2, 3)
    k = np.arange(1, narrow)
    sines = np.sqrt(2.0 / narrow) * np.sin(np.pi * k[:, None] * k[None, :] / narrow)
    table_x = cosine_table(length_x).T.reshape(wide, size_x, length_x)
    f32 = lambda a: np.asarray(a, np.float32)
    return dict(
        group=group,
        z_fwd=pieces(table_z.T),
        z_inv=pieces(table_z, 2),
        y_fwd=pieces(block_y),
        y_inv=pieces(block_y.T, 2),
        decay=f32(decay),
        kappa=f32(kappa),
        powers=f32(powers),
        border=f32(border),
        border_kappa=f32(border * kappa),
        capacity=f32(capacity.reshape(narrow, (narrow - 1) * part_z, length_x)),
        sines=sines,
        table_x=f32(table_x),
    )


def split(values, count):
    result = [values.astype(BF16)]
    rest = values
    for _ in range(count - 1):
        rest = rest - result[-1].astype(F32)
        result.append(rest.astype(BF16))
    return result


def product_right(values, matrix_ref, terms):
    parts = split(values, 1 + max(a for a, _ in terms))
    total = None
    for a, b in reversed(terms):
        term = jnp.dot(parts[a], matrix_ref[b], preferred_element_type=F32)
        total = term if total is None else total + term
    return total


def product_left(matrix_ref, values, terms):
    parts = split(values, 1 + max(a for a, _ in terms))
    total = None
    for a, b in reversed(terms):
        term = jnp.dot(matrix_ref[b], parts[a], preferred_element_type=F32)
        total = term if total is None else total + term
    return total


def lookup(phase, scal, component):
    base = 4 * component
    picked = jnp.where(phase == 2.0, scal[base + 2], scal[base + 3])
    picked = jnp.where(phase == 1.0, scal[base + 1], picked)
    return jnp.where(phase == 0.0, scal[base], picked)


def forward_modes(block, z_ref, y_ref, kappa_ref, decay_ref, modes_ref, ahead_ref, back_ref, power):
    planes, rows, depth = block.shape
    flat = block.reshape(planes * rows, depth)
    flat = product_right(flat, z_ref, FORWARD_TERMS)
    flat = product_left(y_ref, flat, FORWARD_TERMS)
    scaled = flat.reshape(planes, rows, depth) * kappa_ref[...][None]
    modes_ref[...] = scaled
    decay = decay_ref[...]
    ahead, back, weight = (ahead_ref[...], back_ref[...], power[...])
    for j in range(planes):
        ahead = decay * ahead + scaled[j]
        back = back + weight * scaled[j]
        weight = weight * decay
    ahead_ref[...] = ahead
    back_ref[...] = back
    power[...] = weight


def fold(values):
    rows, depth = values.shape
    return jnp.sum(values.reshape(rows // 8, 8, depth), axis=0)


def residual_kernel(
    group, size_x,
    scal, phase_ref, phase_next, field_ref, field_next, x_before, x_after, y_before, y_after,
    z_mat, y_mat, kappa_ref, decay_ref,
    residual_ref, modes_ref, fx_ref, fy_ref, fz_ref, fx_low, fy_low, ahead_ref, back_ref,
    flux_low, power,
):
    step = pl.program_id(0)
    rows, depth = flux_low.shape
    gx, gy, gz = scal[12], scal[13], scal[14]
    flag_xb, flag_xa, flag_yb, flag_ya = scal[15], scal[16], scal[17], scal[18]
    row = lax.broadcasted_iota(jnp.int32, (rows, depth), 0)
    lane = lax.broadcasted_iota(jnp.int32, (rows, depth), 1)

    @pl.when(step == 0)
    def _():
        face = flag_xb / (lookup(x_before[0], scal, 0) + lookup(phase_ref[0].astype(F32), scal, 0))
        fx_low[...] = face
        flux_low[...] = face * (field_ref[0] - x_before[1] + gx)
        ahead_ref[...] = jnp.zeros_like(ahead_ref)
        back_ref[...] = jnp.zeros_like(back_ref)
        power[...] = jnp.ones_like(power)

    last = step == pl.num_programs(0) - 1
    end_phase = jnp.where(last, x_after[0], phase_next[0].astype(F32))
    end_field = jnp.where(last, x_after[1], field_next[0])
    flag_end = jnp.where(last, flag_xa, 1.0)
    flux_x_low = flux_low[...]
    hx = lookup(phase_ref[0].astype(F32), scal, 0)
    for j in range(group):
        x = step * group + j
        phase = phase_ref[j].astype(F32)
        field = field_ref[j]
        if j + 1 < group:
            hx_next = lookup(phase_ref[j + 1].astype(F32), scal, 0)
            field_up = field_ref[j + 1]
            fx = 1.0 / (hx + hx_next)
        else:
            hx_next = lookup(end_phase, scal, 0)
            field_up = end_field
            fx = flag_end / (hx + hx_next)
        flux_x = fx * (field_up - field + gx)
        total = flux_x - flux_x_low
        flux_x_low, hx = flux_x, hx_next
        fx_ref[j] = fx

        hy = lookup(phase, scal, 1)
        hy_up = jnp.where(
            row == rows - 1,
            lookup(y_after[0, pl.ds(x, 1), :], scal, 1),
            pltpu.roll(hy, rows - 1, 0),
        )
        fy = jnp.where(row == rows - 1, flag_ya, 1.0) / (hy + hy_up)
        v_up = jnp.where(row == rows - 1, y_after[1, pl.ds(x, 1), :], pltpu.roll(field, rows - 1, 0))
        flux_y = fy * (v_up - field + gy)
        face = flag_yb / (lookup(y_before[0, pl.ds(x, 1), :], scal, 1) + hy[0:1])
        low = face * (field[0:1] - y_before[1, pl.ds(x, 1), :] + gy)
        total = total + (flux_y - jnp.where(row == 0, low, pltpu.roll(flux_y, 1, 0)))
        fy_ref[j] = fy
        fy_low[pl.ds(x, 1), :] = face

        hz = lookup(phase, scal, 2)
        fz = jnp.where(lane == depth - 1, 0.0, 1.0 / (hz + pltpu.roll(hz, depth - 1, 1)))
        flux_z = fz * (pltpu.roll(field, depth - 1, 1) - field + gz)
        total = total + (flux_z - pltpu.roll(flux_z, 1, 1))
        fz_ref[j] = fz
        residual_ref[j] = total
    flux_low[...] = flux_x_low
    forward_modes(
        residual_ref[...], z_mat, y_mat, kappa_ref, decay_ref, modes_ref, ahead_ref, back_ref, power
    )


def image_kernel(
    group, size_x,
    field_ref, field_next, residual_ref, fx_ref, fy_ref, fz_ref, fx_low, fy_low,
    x_before, x_after, y_before, y_after, z_mat, y_mat, kappa_ref, decay_ref,
    image_ref, modes_ref, ahead_ref, back_ref, sums_ref,
    flux_low, power,
):
    step = pl.program_id(0)
    rows, depth = flux_low.shape
    row = lax.broadcasted_iota(jnp.int32, (rows, depth), 0)

    @pl.when(step == 0)
    def _():
        flux_low[...] = fx_low[...] * (field_ref[0] - x_before[...])
        ahead_ref[...] = jnp.zeros_like(ahead_ref)
        back_ref[...] = jnp.zeros_like(back_ref)
        power[...] = jnp.ones_like(power)
        sums_ref[...] = jnp.zeros_like(sums_ref)

    last = step == pl.num_programs(0) - 1
    end_field = jnp.where(last, x_after[...], field_next[0])
    flux_x_low = flux_low[...]
    sums = [sums_ref[i] for i in range(5)]
    for j in range(group):
        x = step * group + j
        field = field_ref[j]
        field_up = field_ref[j + 1] if j + 1 < group else end_field
        flux_x = fx_ref[j] * (field_up - field)
        total = flux_x_low - flux_x
        flux_x_low = flux_x
        v_up = jnp.where(row == rows - 1, y_after[pl.ds(x, 1), :], pltpu.roll(field, rows - 1, 0))
        flux_y = fy_ref[j] * (v_up - field)
        low = fy_low[pl.ds(x, 1), :] * (field[0:1] - y_before[pl.ds(x, 1), :])
        total = total + (jnp.where(row == 0, low, pltpu.roll(flux_y, 1, 0)) - flux_y)
        flux_z = fz_ref[j] * (pltpu.roll(field, depth - 1, 1) - field)
        total = total + (pltpu.roll(flux_z, 1, 1) - flux_z)
        image_ref[j] = total
        res = residual_ref[j]
        for i, term in enumerate((res * field, res, field * total, total, field)):
            sums[i] = sums[i] + fold(term)
    for i in range(5):
        sums_ref[i] = sums[i]
    flux_low[...] = flux_x_low
    forward_modes(
        image_ref[...], z_mat, y_mat, kappa_ref, decay_ref, modes_ref, ahead_ref, back_ref, power
    )


def incoming(wide, mine, ends_ref, powers_ref, towards):
    total = None
    for block in range(2 * wide):
        mirrored = block >= wide
        source = 2 * wide - 1 - block if mirrored else block
        if towards > 0:
            value = ends_ref[source, 1 if mirrored else 0]
            distance = mine - 1 - block
        else:
            value = ends_ref[source, 0 if mirrored else 1]
            distance = block - 1 - mine
        distance = lax.rem(distance + 4 * wide, 2 * wide)
        term = powers_ref[distance] * value
        total = term if total is None else total + term
    return total


def border_kernel(
    wide, narrow, planes,
    index, modes_ref, ends_ref, powers_ref, decay_ref, border_ref,
    out_ref,
    run, kept, rows_ref,
):
    phase, step = pl.program_id(0), pl.program_id(1)
    blocks = pl.num_programs(1)
    decay = decay_ref[...]
    half = decay.shape[0] // 2

    @pl.when((phase == 0) & (step == 0))
    def _():
        run[...] = incoming(wide, index[0], ends_ref, powers_ref, 1)

    @pl.when(phase == 0)
    def _():
        value = run[...]
        for j in range(planes):
            value = modes_ref[j] + decay * value
            kept[step * planes + j] = value
        run[...] = value

    @pl.when((phase == 1) & (step == 0))
    def _():
        run[...] = incoming(wide, index[0], ends_ref, powers_ref, -1)

    @pl.when(phase == 1)
    def _():
        value = run[...]
        border = border_ref[...]
        first = (blocks - 1 - step) * planes
        for j in reversed(range(planes)):
            passed = decay * value
            mode = (kept[first + j] + passed) * border
            value = modes_ref[j] + passed
            rows_ref[0, pl.ds(first + j, 1), :] = jnp.sum(mode[:half], axis=0, keepdims=True)
            rows_ref[1, pl.ds(first + j, 1), :] = jnp.sum(mode[half:], axis=0, keepdims=True)
        run[...] = value

    @pl.when((phase == 1) & (step == blocks - 1))
    def _():
        part = out_ref.shape[2]
        for side in range(2):
            turned = rows_ref[side].T
            for j in range(narrow):
                out_ref[j, side] = turned[j * part : (j + 1) * part]


def capacity_kernel(wide, narrow, sines, index, jump_ref, table_ref, capacity_ref, out_ref, scratch):
    faces, part, _ = jump_ref.shape[1:]
    mode = None
    for block in range(wide):
        jumps = [jump_ref[block, k] for k in range(faces)]
        for k in range(faces):
            acc = None
            for i in range(faces):
                term = jumps[i] * float(sines[k, i])
                acc = term if acc is None else acc + term
            scratch[pl.ds(k * part, part), :] = acc
        term = jnp.dot(
            scratch[...], table_ref[block], preferred_element_type=F32, precision=lax.Precision.HIGHEST
        )
        mode = term if mode is None else mode + term
    mode = mode * capacity_ref[0]
    scratch[...] = lax.dot_general(
        mode, table_ref[index[0]], (((1,), (1,)), ((), ())),
        preferred_element_type=F32, precision=lax.Precision.HIGHEST,
    )
    solved = []
    for k in range(faces):
        acc = None
        for i in range(faces):
            term = scratch[pl.ds(i * part, part), :] * float(sines[k, i])
            acc = term if acc is None else acc + term
        solved.append(acc)
    for strip in range(narrow):
        if strip == 0:
            even, odd = solved[0], -solved[0]
        elif strip == narrow - 1:
            even, odd = -solved[-1], -solved[-1]
        else:
            even = solved[strip] - solved[strip - 1]
            odd = -(solved[strip] + solved[strip - 1])
        out_ref[strip, 0] = even
        out_ref[strip, 1] = odd


def ends_kernel(narrow, face_ref, ends_ref, decay_ref, scale_ref, out_ref, rows_ref, turned):
    part = face_ref.shape[2]
    for side in range(2):
        for j in range(narrow):
            turned[pl.ds(j * part, part), :] = face_ref[j, side]
        rows_ref[side] = turned[...].T
    size_x = rows_ref.shape[1]
    half = decay_ref.shape[0] // 2
    for side in range(2):
        decay = decay_ref[pl.ds(side * half, half), :]

        def body(x, carry):
            ahead, back = carry
            ahead = decay * ahead + rows_ref[side, pl.ds(x, 1), :]
            back = decay * back + rows_ref[side, pl.ds(size_x - 1 - x, 1), :]
            return ahead, back

        zero = jnp.zeros_like(decay)
        ahead, back = lax.fori_loop(0, size_x, body, (zero, zero), unroll=8)
        scale = scale_ref[pl.ds(side * half, half), :]
        out_ref[0, pl.ds(side * half, half), :] = ends_ref[0, pl.ds(side * half, half), :] + scale * ahead
        out_ref[1, pl.ds(side * half, half), :] = ends_ref[1, pl.ds(side * half, half), :] + scale * back


def inverse_kernel(
    wide, planes, dotted,
    index, modes_ref, ends_ref, powers_ref, decay_ref, scale_ref, rows_ref, y_mat, z_mat, *rest,
):
    if dotted:
        residual_ref, image_ref, out_ref, sums_ref, run, kept, fixed = rest
    else:
        out_ref, first_ref, last_ref, run, kept, fixed = rest
    phase, step = pl.program_id(0), pl.program_id(1)
    blocks = pl.num_programs(1)
    decay = decay_ref[...]
    rows, depth = decay.shape
    half = rows // 2

    @pl.when((phase == 0) & (step == 0))
    def _():
        run[...] = incoming(wide, index[0], ends_ref, powers_ref, 1)

    @pl.when(phase == 0)
    def _():
        value = run[...]
        scale = scale_ref[...]
        for j in range(planes):
            x = step * planes + j
            face = jnp.concatenate(
                [
                    jnp.broadcast_to(rows_ref[0, pl.ds(x, 1), :], (half, depth)),
                    jnp.broadcast_to(rows_ref[1, pl.ds(x, 1), :], (half, depth)),
                ],
                axis=0,
            )
            mode = modes_ref[j] + scale * face
            value = mode + decay * value
            fixed[x] = mode
            kept[x] = value
        run[...] = value

    @pl.when((phase == 1) & (step == 0))
    def _():
        run[...] = incoming(wide, index[0], ends_ref, powers_ref, -1)
        if dotted:
            sums_ref[...] = jnp.zeros_like(sums_ref)

    @pl.when(phase == 1)
    def _():
        value = run[...]
        first = (blocks - 1 - step) * planes
        for j in reversed(range(planes)):
            passed = decay * value
            value = fixed[first + j] + passed
            kept[first + j] = kept[first + j] + passed
        run[...] = value
        flat = kept[pl.ds(first, planes)].reshape(planes * rows, depth)
        flat = product_left(y_mat, flat, INVERSE_TERMS)
        flat = product_right(flat, z_mat, INVERSE_TERMS)
        block = flat.reshape(planes, rows, depth)
        out_ref[...] = block
        if dotted:
            sums = [sums_ref[i] for i in range(3)]
            for j in range(planes):
                for i, term in enumerate((residual_ref[j] * block[j], image_ref[j] * block[j], block[j])):
                    sums[i] = sums[i] + fold(term)
            for i in range(3):
                sums_ref[i] = sums[i]
        else:
            for j in range(planes):
                first_ref[pl.ds(first + j, 1), :] = block[j, 0:1]
                last_ref[pl.ds(first + j, 1), :] = block[j, rows - 1 : rows]


def whole(shape, single=False):
    mode = dict(pipeline_mode=pl.Buffered(1)) if single else {}
    return pl.BlockSpec(shape, lambda *_: (0,) * len(shape), **mode)


def shape_of(*dims):
    return jax.ShapeDtypeStruct(dims, F32)


def params(dims):
    return pltpu.CompilerParams(dimension_semantics=("arbitrary",) * dims, vmem_limit_bytes=VMEM_LIMIT)


def neighbours(axis):
    devices = lax.axis_size(axis)
    up = [(i, i + 1) for i in range(devices - 1)]
    return up, [(j, i) for i, j in up]


def exchange(first, last, axis):
    up, down = neighbours(axis)
    return lax.ppermute(last, axis, up), lax.ppermute(first, axis, down)


def solve(modes, ends, tab, index, kind, extra=()):
    size_x, size_y, size_z = modes.shape
    wide, narrow = lax.axis_size("wide"), lax.axis_size("narrow")
    group = tab["group"]
    blocks = size_x // group
    part = size_z // narrow
    plane = (size_y, size_z)
    wide_at = index[:1]
    sweep = lambda p, i, *_: (jnp.where(p == 0, i, blocks - 1 - i), 0, 0)
    ends_all = lax.all_gather(ends, "wide", axis=0)
    borders = pl.pallas_call(
        functools.partial(border_kernel, wide, narrow, group),
        out_shape=shape_of(narrow, 2, part, size_x),
        grid_spec=pltpu.PrefetchScalarGridSpec(
            num_scalar_prefetch=1,
            grid=(2, blocks),
            in_specs=[
                pl.BlockSpec((group,) + plane, sweep),
                whole((wide, 2) + plane),
                whole((2 * wide,) + plane),
                whole(plane),
                whole(plane),
            ],
            out_specs=whole((narrow, 2, part, size_x)),
            scratch_shapes=[
                pltpu.VMEM(plane, F32),
                pltpu.VMEM((size_x,) + plane, F32),
                pltpu.VMEM((2, size_x, size_z), F32),
            ],
        ),
        compiler_params=params(2),
        name="strip_borders",
    )(wide_at, modes, ends_all, tab["powers"], tab["decay"], tab["border"])
    strips = lax.all_to_all(borders, "narrow", split_axis=0, concat_axis=0, tiled=True)
    jumps = strips[1:, 0] + strips[1:, 1] - strips[:-1, 0] + strips[:-1, 1]
    jumps = lax.all_gather(jumps, "wide", axis=0)
    faces = narrow - 1
    length_x = wide * size_x
    solved = pl.pallas_call(
        functools.partial(capacity_kernel, wide, narrow, tab["sines"]),
        out_shape=shape_of(narrow, 2, part, size_x),
        grid_spec=pltpu.PrefetchScalarGridSpec(
            num_scalar_prefetch=1,
            grid=(1,),
            in_specs=[
                whole((wide, faces, part, size_x)),
                whole((wide, size_x, length_x)),
                pl.BlockSpec((1, faces * part, length_x), lambda i, idx: (idx[1], 0, 0)),
            ],
            out_specs=whole((narrow, 2, part, size_x)),
            scratch_shapes=[pltpu.VMEM((faces * part, size_x), F32)],
        ),
        compiler_params=params(1),
        name="strip_faces",
    )(index, jumps, tab["table_x"], tab["capacity"])
    faces_mine = lax.all_to_all(solved, "narrow", split_axis=0, concat_axis=0, tiled=True)
    ends_fixed, rows = pl.pallas_call(
        functools.partial(ends_kernel, narrow),
        out_shape=(shape_of(2, *plane), shape_of(2, size_x, size_z)),
        in_specs=[pl.BlockSpec(memory_space=pltpu.VMEM)] * 4,
        out_specs=(pl.BlockSpec(memory_space=pltpu.VMEM),) * 2,
        scratch_shapes=[pltpu.VMEM((size_z, size_x), F32)],
        compiler_params=pltpu.CompilerParams(vmem_limit_bytes=VMEM_LIMIT),
        name="block_ends",
    )(faces_mine, ends, tab["decay"], tab["border_kappa"])
    ends_all = lax.all_gather(ends_fixed, "wide", axis=0)
    dotted = bool(extra)
    back = lambda p, i, *_: (jnp.where(p == 0, blocks - 1, blocks - 1 - i), 0, 0)
    ahead = lambda p, i, *_: (jnp.where(p == 0, i, blocks - 1), 0, 0)
    block = (group,) + plane
    if dotted:
        out_shape = (shape_of(size_x, *plane), shape_of(3, 8, size_z))
        out_specs = (pl.BlockSpec(block, back), whole((3, 8, size_z)))
    else:
        out_shape = (shape_of(size_x, *plane),) + (shape_of(size_x, size_z),) * 2
        out_specs = (pl.BlockSpec(block, back),) + (whole((size_x, size_z)),) * 2
    return pl.pallas_call(
        functools.partial(inverse_kernel, wide, group, dotted),
        out_shape=out_shape,
        grid_spec=pltpu.PrefetchScalarGridSpec(
            num_scalar_prefetch=1,
            grid=(2, blocks),
            in_specs=[
                pl.BlockSpec(block, ahead),
                whole((wide, 2) + plane),
                whole((2 * wide,) + plane),
                whole(plane),
                whole(plane),
                whole((2, size_x, size_z)),
                whole(tab["y_inv"].shape),
                whole(tab["z_inv"].shape),
            ]
            + [pl.BlockSpec(block, back)] * len(extra),
            out_specs=out_specs,
            scratch_shapes=[
                pltpu.VMEM(plane, F32),
                pltpu.VMEM((size_x,) + plane, F32),
                pltpu.VMEM((size_x,) + plane, F32),
            ],
        ),
        compiler_params=params(2),
        name="inverse_modes",
    )(
        wide_at, modes, ends_all, tab["powers"], tab["decay"], tab["border_kappa"], rows,
        tab["y_inv"], tab["z_inv"], *extra,
    )


def on_device(phase_ids, conduct_table, gradient, start_field):
    size_x, size_y, size_z = start_field.shape
    wide, narrow = lax.axis_size("wide"), lax.axis_size("narrow")
    tab = make_tables(size_x, size_y, size_z, wide, narrow)
    tab = {k: jnp.asarray(v) if isinstance(v, np.ndarray) and k != "sines" else v for k, v in tab.items()}
    group = tab["group"]
    blocks = size_x // group
    plane = (size_y, size_z)
    block = (group,) + plane
    wide_at, narrow_at = lax.axis_index("wide"), lax.axis_index("narrow")
    index = jnp.stack([wide_at, narrow_at]).astype(jnp.int32)
    flags = jnp.stack([wide_at > 0, wide_at < wide - 1, narrow_at > 0, narrow_at < narrow - 1])
    scal = jnp.concatenate([(0.5 / conduct_table).T.reshape(-1), gradient, flags.astype(F32)])
    kappa = tab["kappa"] / jnp.mean(conduct_table)

    edge = lambda dim, at: jnp.stack(
        [lax.index_in_dim(phase_ids, at, dim, False).astype(F32), lax.index_in_dim(start_field, at, dim, False)]
    )
    x_before, x_after = exchange(edge(0, 0), edge(0, size_x - 1), "wide")
    y_before, y_after = exchange(edge(1, 0), edge(1, size_y - 1), "narrow")

    main = pl.BlockSpec(block, lambda i: (i, 0, 0))
    following = pl.BlockSpec((1,) + plane, lambda i: (jnp.minimum((i + 1) * group, size_x - 1), 0, 0))
    field_shape = shape_of(size_x, *plane)
    matrices = [whole(tab["z_fwd"].shape), whole(tab["y_fwd"].shape), whole(plane), whole(plane)]
    carried = [pltpu.VMEM(plane, F32), pltpu.VMEM(plane, F32)]
    residual, modes, fx, fy, fz, fx_low, fy_low, ahead, back = pl.pallas_call(
        functools.partial(residual_kernel, group, size_x),
        grid=(blocks,),
        out_shape=(field_shape,) * 5 + (shape_of(*plane), shape_of(size_x, size_z)) + (shape_of(*plane),) * 2,
        in_specs=[pl.BlockSpec(memory_space=pltpu.SMEM), main, following, main, following]
        + [whole((2,) + plane)] * 2
        + [whole((2, size_x, size_z))] * 2
        + matrices,
        out_specs=(main,) * 5 + (whole(plane), whole((size_x, size_z))) + (whole(plane),) * 2,
        scratch_shapes=carried,
        compiler_params=params(1),
        name="residual_modes",
    )(
        scal, phase_ids, phase_ids, start_field, start_field, x_before, x_after, y_before, y_after,
        tab["z_fwd"], tab["y_fwd"], kappa, tab["decay"],
    )
    along, row_first, row_last = solve(modes, jnp.stack([ahead, back]), tab, index, 0)

    xb, xa = exchange(along[0], along[size_x - 1], "wide")
    yb, ya = exchange(row_first, row_last, "narrow")
    image, modes, ahead, back, sums = pl.pallas_call(
        functools.partial(image_kernel, group, size_x),
        grid=(blocks,),
        out_shape=(field_shape,) * 2 + (shape_of(*plane),) * 2 + (shape_of(5, 8, size_z),),
        in_specs=[main, following] + [main] * 4
        + [whole(plane), whole((size_x, size_z))]
        + [whole(plane)] * 2
        + [whole((size_x, size_z))] * 2
        + matrices,
        out_specs=(main,) * 2 + (whole(plane),) * 2 + (whole((5, 8, size_z)),),
        scratch_shapes=carried,
        compiler_params=params(1),
        name="image_modes",
    )(
        along, along, residual, fx, fy, fz, fx_low, fy_low, xb, xa, yb, ya,
        tab["z_fwd"], tab["y_fwd"], kappa, tab["decay"],
    )
    turned, sums_late = solve(modes, jnp.stack([ahead, back]), tab, index, 1, (residual, image))

    sums = jnp.concatenate([jnp.sum(sums, axis=(1, 2)), jnp.sum(sums_late, axis=(1, 2))])
    sums = lax.psum(lax.psum(sums, "narrow"), "wide")
    res_along, res_one, along_image, image_one, along_one, res_turned, image_turned, turned_one = [
        sums[i] for i in range(8)
    ]
    voxels = float(size_x * wide * size_y * narrow * size_z)
    mean_along = along_one / voxels
    mean_turned = turned_one / voxels
    rz_now = res_along - mean_along * res_one
    curvature = along_image - mean_along * image_one
    alpha = rz_now / curvature
    cross = res_turned - mean_turned * res_one
    square = image_turned - mean_turned * image_one
    rz_next = rz_now - alpha * (cross + curvature) + alpha * (alpha * square)
    beta = rz_next / rz_now
    direction = along - mean_along
    return (
        start_field + alpha * direction,
        residual - alpha * image,
        direction * (1.0 + beta) - alpha * (turned - mean_turned),
    )


def solution(mesh):
    placed = (P("wide", "narrow", None), P(), P(), P("wide", "narrow", None))
    return jax.shard_map(
        on_device,
        mesh=mesh,
        in_specs=placed,
        out_specs=(P("wide", "narrow", None),) * 3,
        check_vma=False,
    )
```

```python
import functools

import jax
import jax.numpy as jnp
import ml_dtypes
import numpy as np
from jax import lax
from jax.experimental import pallas as pl
from jax.experimental.pallas import tpu as pltpu
from jax.sharding import PartitionSpec as P

PHASES = 4
F32 = jnp.float32
BF16 = jnp.bfloat16
VMEM_LIMIT = 56 * 1024 * 1024
PLANES = 16
FORWARD_TERMS = ((0, 0), (0, 1), (1, 0), (1, 1), (0, 2), (2, 0))
INVERSE_TERMS = ((0, 0), (0, 1), (1, 0))


def cosine_table(length):
    m = np.arange(length)[:, None]
    n = np.arange(length)[None, :]
    weight = np.where(m == 0, np.sqrt(1.0 / length), np.sqrt(2.0 / length))
    return weight * np.cos(np.pi * (m * (2 * n + 1) % (4 * length)) / (2.0 * length))


def eigen_values(length):
    return 4.0 * np.sin(np.pi * np.arange(length) / (2.0 * length)) ** 2


def pieces(matrix, count=3):
    rest = np.asarray(matrix, np.float64)
    result = []
    for _ in range(count):
        piece = rest.astype(np.float32).astype(ml_dtypes.bfloat16)
        result.append(piece)
        rest = rest - piece.astype(np.float64)
    return np.stack(result)


def make_tables(size_x, size_y, size_z, wide, narrow):
    length_x = size_x * wide
    group = min(max(256 // size_y, 1), size_x)
    parity = np.concatenate([np.arange(0, size_y, 2), np.arange(1, size_y, 2)])
    strip = cosine_table(size_y)[parity]
    block_y = np.kron(np.eye(group), strip)
    table_z = cosine_table(size_z)
    shift = 4.0 * np.sin(np.pi / (2.0 * length_x)) ** 2
    eig_z = eigen_values(size_z)
    sigma = shift + eigen_values(size_y)[parity][:, None] + eig_z[None, :]
    theta = 2.0 * np.arcsinh(np.sqrt(sigma) / 2.0)
    decay = np.exp(-theta)
    kappa = 1.0 / (2.0 * np.sinh(theta))
    step = np.exp(-theta * size_x)
    total = -np.expm1(-2.0 * wide * size_x * theta)
    powers = np.stack([step**t / total for t in range(2 * wide)])
    border = np.broadcast_to(strip[:, :1], sigma.shape)
    eta = 2.0 * np.arcsinh(
        np.sqrt(shift + eig_z[:, None] + eigen_values(length_x)[None, :]) / 2.0
    )
    fade = np.exp(-eta * size_y)
    half_angle = np.pi * np.arange(1, narrow) / (2.0 * narrow)
    capacity = (np.tanh(eta / 2.0) * -np.expm1(-2.0 * eta * size_y))[None] / (
        (np.expm1(-eta * size_y) ** 2)[None]
        + 4.0 * fade[None] * (np.sin(half_angle) ** 2)[:, None, None]
    )
    devices = wide * narrow
    part = size_z // devices
    capacity = capacity.reshape(narrow - 1, devices, part, length_x).transpose(1, 0, 2, 3)
    k = np.arange(1, narrow)
    sines = np.sqrt(2.0 / narrow) * np.sin(np.pi * k[:, None] * k[None, :] / narrow)
    table_x = cosine_table(length_x).T.reshape(wide, size_x, length_x)
    by_mode = lambda left, right: np.concatenate([left.T, right.T], axis=1).reshape(devices, part, 2 * size_y)
    mix = np.stack(
        [
            np.stack(
                [
                    np.stack(
                        [
                            by_mode(powers[(d - 1 - b) % (2 * wide)], powers[(b - 1 - d) % (2 * wide)]),
                            by_mode(powers[(d + b) % (2 * wide)], powers[(2 * wide - 2 - b - d) % (2 * wide)]),
                        ],
                        axis=1,
                    )
                    for b in range(wide)
                ],
                axis=1,
            )
            for d in range(wide)
        ],
        axis=1,
    )
    even = np.broadcast_to((np.arange(size_y) < (size_y + 1) // 2)[:, None], sigma.shape)
    row, end = (border * decay, border * kappa)
    twice = lambda values: by_mode(values, values)
    f32 = lambda a: np.asarray(a, np.float32)
    return dict(
        group=group,
        planes=min(PLANES, size_x),
        z_fwd=pieces(table_z.T),
        z_inv=pieces(table_z, 2),
        y_fwd=pieces(block_y),
        y_inv=pieces(block_y.T, 2),
        theta=f32(theta.T.reshape(devices, part, size_y)),
        decay=f32(decay),
        kappa=f32(kappa),
        border=f32(border),
        border_kappa=f32(end),
        mix=f32(mix),
        row_even=f32(twice(np.where(even, row, 0.0))),
        row_odd=f32(twice(np.where(even, 0.0, row))),
        row_dot=f32(twice(decay / kappa)),
        inverse_kappa=f32(1.0 / kappa),
        mean_scale=float(np.sqrt(size_y * size_z) / (shift * kappa[0, 0])),
        end_even=f32(twice(np.where(even, end, 0.0))),
        end_odd=f32(twice(np.where(even, 0.0, end))),
        capacity=f32(capacity.reshape(devices, (narrow - 1) * part, length_x)),
        sines=sines,
        table_x=f32(table_x),
    )


def split(values, count):
    result = [values.astype(BF16)]
    rest = values
    for _ in range(count - 1):
        rest = rest - result[-1].astype(F32)
        result.append(rest.astype(BF16))
    return result


def product_right(values, matrix_ref, terms):
    parts = split(values, 1 + max(a for a, _ in terms))
    total = None
    for a, b in reversed(terms):
        term = jnp.dot(parts[a], matrix_ref[b], preferred_element_type=F32)
        total = term if total is None else total + term
    return total


def product_left(matrix_ref, values, terms):
    parts = split(values, 1 + max(a for a, _ in terms))
    total = None
    for a, b in reversed(terms):
        term = jnp.dot(matrix_ref[b], parts[a], preferred_element_type=F32)
        total = term if total is None else total + term
    return total


def lookup(phase, scal, component):
    base = 4 * component
    picked = jnp.where(phase == 2.0, scal[base + 2], scal[base + 3])
    picked = jnp.where(phase == 1.0, scal[base + 1], picked)
    return jnp.where(phase == 0.0, scal[base], picked)


def forward_modes(first, block, z_ref, y_ref, kappa_ref, decay_ref, modes_ref, ahead_ref, back_ref, power):
    rows = block[0].shape[0]
    flat = jnp.concatenate(block, axis=0)
    flat = product_right(flat, z_ref, FORWARD_TERMS)
    flat = product_left(y_ref, flat, FORWARD_TERMS)
    kappa, decay = (kappa_ref[...], decay_ref[...])
    ahead, back, weight = (ahead_ref[...], back_ref[...], power[...])
    for j in range(len(block)):
        scaled = flat[j * rows : (j + 1) * rows] * kappa
        modes_ref[first + j] = scaled
        ahead = decay * ahead + scaled
        back = back + weight * scaled
        weight = weight * decay
    ahead_ref[...] = ahead
    back_ref[...] = back
    power[...] = weight


def fold(values):
    rows, depth = values.shape
    return jnp.sum(values.reshape(rows // 8, 8, depth), axis=0)


def residual_kernel(
    group, planes,
    scal, phase_ref, phase_next, field_ref, field_next, x_before, x_after, y_before, y_after,
    z_mat, y_mat, kappa_ref, decay_ref,
    residual_ref, modes_ref, fx_ref, fy_ref, fz_ref, fx_low, fy_low, ahead_ref, back_ref,
    flux_low, power,
):
    step = pl.program_id(0)
    rows, depth = flux_low.shape
    gx, gy, gz = scal[12], scal[13], scal[14]
    flag_xb, flag_xa, flag_yb, flag_ya = scal[15], scal[16], scal[17], scal[18]
    row = lax.broadcasted_iota(jnp.int32, (rows, depth), 0)
    lane = lax.broadcasted_iota(jnp.int32, (rows, depth), 1)

    @pl.when(step == 0)
    def _():
        face = flag_xb / (lookup(x_before[0], scal, 0) + lookup(phase_ref[0].astype(F32), scal, 0))
        fx_low[...] = face
        flux_low[...] = face * (field_ref[0] - x_before[1] + gx)
        ahead_ref[...] = jnp.zeros_like(ahead_ref)
        back_ref[...] = jnp.zeros_like(back_ref)
        power[...] = jnp.ones_like(power)

    last = step == pl.num_programs(0) - 1
    end_phase = jnp.where(last, x_after[0], phase_next[0].astype(F32))
    end_field = jnp.where(last, x_after[1], field_next[0])
    flag_end = jnp.where(last, flag_xa, 1.0)
    flux_x_low = flux_low[...]
    hx = lookup(phase_ref[0].astype(F32), scal, 0)
    done = []
    for j in range(planes):
        x = step * planes + j
        phase = phase_ref[j].astype(F32)
        field = field_ref[j]
        if j + 1 < planes:
            hx_next = lookup(phase_ref[j + 1].astype(F32), scal, 0)
            field_up = field_ref[j + 1]
            fx = 1.0 / (hx + hx_next)
        else:
            hx_next = lookup(end_phase, scal, 0)
            field_up = end_field
            fx = flag_end / (hx + hx_next)
        flux_x = fx * (field_up - field + gx)
        total = flux_x - flux_x_low
        flux_x_low, hx = flux_x, hx_next
        fx_ref[j] = fx

        hy = lookup(phase, scal, 1)
        hy_up = jnp.where(
            row == rows - 1,
            lookup(y_after[0, pl.ds(x, 1), :], scal, 1),
            pltpu.roll(hy, rows - 1, 0),
        )
        fy = jnp.where(row == rows - 1, flag_ya, 1.0) / (hy + hy_up)
        v_up = jnp.where(row == rows - 1, y_after[1, pl.ds(x, 1), :], pltpu.roll(field, rows - 1, 0))
        flux_y = fy * (v_up - field + gy)
        face = flag_yb / (lookup(y_before[0, pl.ds(x, 1), :], scal, 1) + hy[0:1])
        low = face * (field[0:1] - y_before[1, pl.ds(x, 1), :] + gy)
        total = total + (flux_y - jnp.where(row == 0, low, pltpu.roll(flux_y, 1, 0)))
        fy_ref[j] = fy
        fy_low[pl.ds(x, 1), :] = face

        hz = lookup(phase, scal, 2)
        fz = jnp.where(lane == depth - 1, 0.0, 1.0 / (hz + pltpu.roll(hz, depth - 1, 1)))
        flux_z = fz * (pltpu.roll(field, depth - 1, 1) - field + gz)
        total = total + (flux_z - pltpu.roll(flux_z, 1, 1))
        fz_ref[j] = fz
        residual_ref[j] = total
        done.append(total)
        if len(done) == group:
            forward_modes(
                j + 1 - group, done, z_mat, y_mat, kappa_ref, decay_ref, modes_ref, ahead_ref, back_ref, power
            )
            done = []
    flux_low[...] = flux_x_low


def image_kernel(
    group, planes,
    field_ref, field_next, residual_ref, fx_ref, fy_ref, fz_ref, fx_low, fy_low,
    x_before, x_after, y_jump, z_mat, y_mat, kappa_ref, decay_ref,
    image_ref, modes_ref, ahead_ref, back_ref, sums_ref,
    flux_low, power,
):
    step = pl.program_id(0)
    rows, depth = flux_low.shape
    row = lax.broadcasted_iota(jnp.int32, (rows, depth), 0)

    @pl.when(step == 0)
    def _():
        flux_low[...] = fx_low[...] * (field_ref[0] - x_before[...])
        ahead_ref[...] = jnp.zeros_like(ahead_ref)
        back_ref[...] = jnp.zeros_like(back_ref)
        power[...] = jnp.ones_like(power)
        sums_ref[...] = jnp.zeros_like(sums_ref)

    last = step == pl.num_programs(0) - 1
    end_field = jnp.where(last, x_after[...], field_next[0])
    flux_x_low = flux_low[...]
    sums = [sums_ref[i] for i in range(5)]
    done = []
    for j in range(planes):
        x = step * planes + j
        field = field_ref[j]
        field_up = field_ref[j + 1] if j + 1 < planes else end_field
        flux_x = fx_ref[j] * (field_up - field)
        total = flux_x_low - flux_x
        flux_x_low = flux_x
        jump = jnp.where(row == rows - 1, y_jump[1, pl.ds(x, 1), :], pltpu.roll(field, rows - 1, 0) - field)
        flux_y = fy_ref[j] * jump
        low = fy_low[pl.ds(x, 1), :] * y_jump[0, pl.ds(x, 1), :]
        total = total + (jnp.where(row == 0, low, pltpu.roll(flux_y, 1, 0)) - flux_y)
        flux_z = fz_ref[j] * (pltpu.roll(field, depth - 1, 1) - field)
        total = total + (pltpu.roll(flux_z, 1, 1) - flux_z)
        image_ref[j] = total
        res = residual_ref[j]
        for i, term in enumerate((res * field, res, field * total, total, field)):
            sums[i] = sums[i] + fold(term)
        done.append(total)
        if len(done) == group:
            forward_modes(
                j + 1 - group, done, z_mat, y_mat, kappa_ref, decay_ref, modes_ref, ahead_ref, back_ref, power
            )
            done = []
    for i in range(5):
        sums_ref[i] = sums[i]
    flux_low[...] = flux_x_low


def local_kernel(devices, planes, summed, modes_ref, ahead_ref, back_ref, decay_ref, border_ref, *rest):
    if summed:
        sums_ref, weight_ref, out_ref, run, kept, rows_ref, dots, corner = rest
    else:
        out_ref, run, kept, rows_ref = rest
    phase, step = pl.program_id(0), pl.program_id(1)
    blocks = pl.num_programs(1)
    decay = decay_ref[...]
    half = decay.shape[0] // 2

    @pl.when(step == 0)
    def _():
        run[...] = jnp.zeros_like(run)
        if summed:
            dots[...] = jnp.zeros_like(dots)

    @pl.when(phase == 0)
    def _():
        value = run[...]
        for j in range(planes):
            value = modes_ref[j] + decay * value
            kept[step * planes + j] = value
        run[...] = value
        if summed:
            lowest = modes_ref[0, :8, :128]
            for j in range(1, planes):
                lowest = lowest + modes_ref[j, :8, :128]
            corner[...] = jnp.where(step == 0, lowest, corner[...] + lowest)

    @pl.when(phase == 1)
    def _():
        value = run[...]
        border = border_ref[...]
        first = (blocks - 1 - step) * planes
        total = dots[...] if summed else None
        for j in reversed(range(planes)):
            passed = decay * value
            mode = kept[first + j] + passed
            if summed:
                total = total + modes_ref[j] * mode
            mode = mode * border
            value = modes_ref[j] + passed
            rows_ref[0, pl.ds(first + j, 1), :] = jnp.sum(mode[:half], axis=0, keepdims=True)
            rows_ref[1, pl.ds(first + j, 1), :] = jnp.sum(mode[half:], axis=0, keepdims=True)
        run[...] = value
        if summed:
            dots[...] = total

    @pl.when((phase == 1) & (step == blocks - 1))
    def _():
        part, width = out_ref.shape[2:]
        ends = jnp.concatenate([ahead_ref[...], back_ref[...]], axis=0)
        for slot, turned in enumerate((rows_ref[0].T, rows_ref[1].T, ends.T)):
            for j in range(devices):
                out_ref[j, slot] = turned[j * part : (j + 1) * part]
        if summed:
            lane = lax.broadcasted_iota(jnp.int32, (part, width), 1)
            packed = jnp.zeros((part, width), F32)
            for i in range(5):
                packed = jnp.where(lane == i, jnp.sum(sums_ref[i]), packed)
            packed = jnp.where(lane == 5, jnp.sum(dots[...] * weight_ref[...]), packed)
            packed = jnp.where(lane == 6, jnp.sum(corner[:1, :1]), packed)
            for j in range(devices):
                out_ref[j, 3] = packed


def faces_kernel(
    wide, narrow, part, sines, summed,
    device, got_ref, table_ref, capacity_ref, power_ref, mix_ref, row_even, row_odd, end_even, end_odd, row_dot,
    out_ref, jumps, modes,
):
    devices = wide * narrow
    width = got_ref.shape[1]
    slots = 4 if summed else 3
    faces = narrow - 1
    highest = dict(preferred_element_type=F32, precision=lax.Precision.HIGHEST)

    def take(ref, slot, mode, count):
        return ref[pl.ds(slot * part + mode, devices, stride=count * part), :]

    def incoming(ends, mode):
        swapped = pltpu.roll(ends, width // 2, 1)
        result = []
        for mine in range(wide):
            total = None
            for block in range(wide):
                at = slice(block * narrow, (block + 1) * narrow)
                term = mix_ref[0, mine, block, 0, pl.ds(mode, 1), :] * ends[at]
                term = term + mix_ref[0, mine, block, 1, pl.ds(mode, 1), :] * swapped[at]
                total = term if total is None else total + term
            result.append(total)
        return jnp.concatenate(result, axis=0)

    inner = None
    for mode in range(part):
        ends = take(got_ref, 2, mode, slots)
        entering = incoming(ends, mode)
        if summed:
            term = entering * pltpu.roll(ends, width // 2, 1) * row_dot[0, pl.ds(mode, 1), :]
            inner = term if inner is None else inner + term
        both = jnp.concatenate(
            [entering * row_even[0, pl.ds(mode, 1), :], entering * row_odd[0, pl.ds(mode, 1), :]], axis=0
        )
        added = jnp.dot(both, power_ref[mode], **highest)
        even = take(got_ref, 0, mode, slots) + added[:devices]
        odd = take(got_ref, 1, mode, slots) + added[devices:]
        jump = pltpu.roll(even + odd, devices - 1, 0) - (even - odd)
        jumps[pl.ds(mode, devices, stride=part), :] = jump
    mixed = None
    for block in range(wide):
        strips = [jumps[pl.ds((block * narrow + i) * part, part), :] for i in range(faces)]
        for k in range(faces):
            acc = None
            for i in range(faces):
                term = strips[i] * float(sines[k, i])
                acc = term if acc is None else acc + term
            modes[pl.ds(k * part, part), :] = acc
        term = jnp.dot(modes[...], table_ref[block], **highest)
        mixed = term if mixed is None else mixed + term
    plain = mixed
    mixed = mixed * capacity_ref[0]
    for block in range(wide):
        modes[...] = lax.dot_general(mixed, table_ref[block], (((1,), (1,)), ((), ())), **highest)
        solved = []
        for k in range(faces):
            acc = None
            for i in range(faces):
                term = modes[pl.ds(i * part, part), :] * float(sines[k, i])
                acc = term if acc is None else acc + term
            solved.append(acc)
        for strip in range(narrow):
            below = solved[strip - 1] if strip > 0 else jnp.zeros_like(solved[0])
            above = solved[strip] if strip < faces else jnp.zeros_like(solved[0])
            at = (block * narrow + strip) * slots * part
            out_ref[pl.ds(at, part), :] = above - below
            out_ref[pl.ds(at + part, part), :] = -(above + below)
    for mode in range(part):
        both = jnp.concatenate([take(out_ref, 0, mode, slots), take(out_ref, 1, mode, slots)], axis=0)
        added = lax.dot_general(both, power_ref[mode], (((1,), (1,)), ((), ())), **highest)
        added = pltpu.roll(added, width // 2, 1)
        ends = take(got_ref, 2, mode, slots) + end_even[0, pl.ds(mode, 1), :] * added[:devices]
        ends = ends + end_odd[0, pl.ds(mode, 1), :] * added[devices:]
        out_ref[pl.ds(2 * part + mode, devices, stride=slots * part), :] = incoming(ends, mode)
    if summed:
        totals = jnp.sum(take(got_ref, 3, 0, slots), axis=0, keepdims=True)
        share = jnp.sum(inner) - jnp.sum(plain * mixed)
        lane = lax.broadcasted_iota(jnp.int32, (part, width), 1)
        packed = jnp.where(lane == 7, share, jnp.broadcast_to(totals, (part, width)))
        for j in range(devices):
            out_ref[pl.ds((j * slots + 3) * part, part), :] = packed


def inverse_kernel(
    group, planes, dotted, voxels, mean_scale,
    faces_ref, modes_ref, decay_ref, scale_ref, y_mat, z_mat, *rest,
):
    if dotted:
        scal, residual_ref, image_ref, along_ref, start_ref = rest[:5]
        out_ref, solution_ref, next_ref = rest[5:8]
    else:
        out_ref, before_ref, after_ref, jump_ref = rest[:4]
    run, kept, fixed, rows_ref, entering, turned, factors = rest[-7:]
    phase, step = pl.program_id(0), pl.program_id(1)
    blocks = pl.num_programs(1)
    decay = decay_ref[...]
    rows, depth = decay.shape
    half = rows // 2

    @pl.when((phase == 0) & (step == 0))
    def _():
        devices, _, part, _ = faces_ref.shape
        for slot in range(3):
            for j in range(devices):
                turned[pl.ds(j * part, part), :] = faces_ref[j, slot]
            if slot < 2:
                rows_ref[slot] = turned[...].T
            else:
                entering[...] = turned[...].T
        run[...] = entering[pl.ds(0, rows), :]
        if dotted:
            shared = faces_ref[0, 3]
            for j in range(1, devices):
                shared = shared + faces_ref[j, 3]
            lane = lax.broadcasted_iota(jnp.int32, shared.shape, 1)[:1]

            def value(i):
                source = shared if i == 7 else faces_ref[0, 3]
                return jnp.sum(jnp.where(lane == i, source[:1], 0.0), axis=1, keepdims=True)

            base = scal[0]
            mean = value(4) / voxels
            mean_turned = value(6) * (mean_scale / voxels)
            rz_now = value(0) - mean * value(1)
            alpha = rz_now / (value(2) - mean * value(3))
            square = base * (value(5) + value(7)) - mean_turned * value(3)
            ratio = alpha * (alpha * square) / rz_now
            for i, factor in enumerate((alpha, mean, ratio, ratio * mean - alpha * mean_turned)):
                factors[pl.ds(i, 1), :] = jnp.broadcast_to(factor, (1, depth))

    @pl.when(phase == 0)
    def _():
        value = run[...]
        scale = scale_ref[...]
        for j in range(planes):
            x = step * planes + j
            face = jnp.concatenate(
                [
                    jnp.broadcast_to(rows_ref[0, pl.ds(x, 1), :], (half, depth)),
                    jnp.broadcast_to(rows_ref[1, pl.ds(x, 1), :], (half, depth)),
                ],
                axis=0,
            )
            mode = modes_ref[j] + scale * face
            value = mode + decay * value
            fixed[x] = mode
            kept[x] = value
        run[...] = value

    @pl.when((phase == 1) & (step == 0))
    def _():
        run[...] = entering[pl.ds(rows, rows), :]

    @pl.when(phase == 1)
    def _():
        value = run[...]
        first = (blocks - 1 - step) * planes
        if dotted:
            alpha, mean, ratio, offset = [
                jnp.broadcast_to(factors[pl.ds(i, 1), :], (rows, depth)) for i in range(4)
            ]
        for start in reversed(range(0, planes, group)):
            modes = [None] * group
            for j in reversed(range(group)):
                x = first + start + j
                passed = decay * value
                value = fixed[x] + passed
                modes[j] = kept[x] + passed
            flat = jnp.concatenate(modes, axis=0)
            flat = product_left(y_mat, flat, INVERSE_TERMS)
            flat = product_right(flat, z_mat, INVERSE_TERMS)
            for j in range(group):
                at = start + j
                plane = flat[j * rows : (j + 1) * rows]
                if dotted:
                    along = along_ref[at]
                    next_ref[at] = residual_ref[at] - alpha * image_ref[at]
                    solution_ref[at] = start_ref[at] + alpha * (along - mean)
                    plane = (ratio * along - offset) - alpha * plane
                out_ref[at] = plane
        run[...] = value

    if not dotted:
        @pl.when((phase == 1) & (step == blocks - 1))
        def _():
            before = entering[pl.ds(0, rows), :] + decay * run[...]
            after = entering[pl.ds(rows, rows), :] + decay * kept[blocks * planes - 1]
            flat = jnp.concatenate([before, after] * (group // 2), axis=0)
            flat = product_left(y_mat, flat, INVERSE_TERMS)
            flat = product_right(flat, z_mat, INVERSE_TERMS)
            before_ref[...] = flat[:rows]
            after_ref[...] = flat[rows : 2 * rows]
            jump_ref[0] = product_right(-0.5 * (rows_ref[0] + rows_ref[1]), z_mat, INVERSE_TERMS)
            jump_ref[1] = product_right(0.5 * (rows_ref[0] - rows_ref[1]), z_mat, INVERSE_TERMS)


def whole(shape, single=False):
    mode = dict(pipeline_mode=pl.Buffered(1)) if single else {}
    return pl.BlockSpec(shape, lambda *_: (0,) * len(shape), **mode)


def shape_of(*dims):
    return jax.ShapeDtypeStruct(dims, F32)


def params(dims):
    return pltpu.CompilerParams(dimension_semantics=("arbitrary",) * dims, vmem_limit_bytes=VMEM_LIMIT)


def neighbours(axis):
    devices = lax.axis_size(axis)
    up = [(i, i + 1) for i in range(devices - 1)]
    return up, [(j, i) for i, j in up]


def exchange(first, last, axis):
    up, down = neighbours(axis)
    return lax.ppermute(last, axis, up), lax.ppermute(first, axis, down)


def solve(modes, ahead, back, tab, device, sums=None, final=None):
    size_x, size_y, size_z = modes.shape
    wide, narrow = lax.axis_size("wide"), lax.axis_size("narrow")
    devices = wide * narrow
    group, planes = tab["group"], tab["planes"]
    blocks = size_x // planes
    part = size_z // devices
    plane = (size_y, size_z)
    block = (planes,) + plane
    summed = sums is not None
    slots = 4 if summed else 3
    field = shape_of(size_x, *plane)
    sweep = lambda p, i, *_: (jnp.where(p == 0, i, blocks - 1 - i), 0, 0)
    packed = (devices, slots, part, size_x)
    sent = pl.pallas_call(
        functools.partial(local_kernel, devices, planes, summed),
        grid=(2, blocks),
        out_shape=shape_of(*packed),
        in_specs=[pl.BlockSpec(block, sweep)]
        + [whole(plane)] * 4
        + [whole((5, 8, size_z)), whole(plane)] * summed,
        out_specs=whole(packed),
        scratch_shapes=[
            pltpu.VMEM(plane, F32),
            pltpu.VMEM((size_x,) + plane, F32),
            pltpu.VMEM((2, size_x, size_z), F32),
        ]
        + [pltpu.VMEM(plane, F32), pltpu.VMEM((8, 128), F32)] * summed,
        compiler_params=params(2),
        name="strip_borders",
    )(modes, ahead, back, tab["decay"], tab["border"], *([sums, tab["inverse_kappa"]] if summed else []))
    got = lax.all_to_all(sent, ("wide", "narrow"), split_axis=0, concat_axis=0, tiled=True)
    faces = narrow - 1
    length_x = wide * size_x
    flat = (devices * slots * part, size_x)
    mine = lambda shape: pl.BlockSpec((1,) + shape, lambda i, idx: (idx[0],) + (0,) * len(shape))
    solved = pl.pallas_call(
        functools.partial(faces_kernel, wide, narrow, part, tab["sines"], summed),
        out_shape=shape_of(*flat),
        grid_spec=pltpu.PrefetchScalarGridSpec(
            num_scalar_prefetch=1,
            grid=(1,),
            in_specs=[
                whole(flat),
                whole((wide, size_x, length_x)),
                mine((faces * part, length_x)),
                whole((part, 2 * size_y, size_x)),
                mine((wide, wide, 2, part, size_x)),
            ]
            + [mine((part, size_x))] * 5,
            out_specs=whole(flat),
            scratch_shapes=[
                pltpu.VMEM((devices * part, size_x), F32),
                pltpu.VMEM((faces * part, size_x), F32),
            ],
        ),
        compiler_params=params(1),
        name="strip_faces",
    )(
        device, got.reshape(flat), tab["table_x"], tab["capacity"], tab["decay_powers"], tab["mix"],
        tab["row_even"], tab["row_odd"], tab["end_even"], tab["end_odd"], tab["row_dot"],
    )
    mine_now = lax.all_to_all(
        solved.reshape(packed), ("wide", "narrow"), split_axis=0, concat_axis=0, tiled=True
    )
    back_map = lambda p, i, *_: (jnp.where(p == 0, blocks - 1, blocks - 1 - i), 0, 0)
    ahead_map = lambda p, i, *_: (jnp.where(p == 0, i, blocks - 1), 0, 0)
    behind = pl.BlockSpec(block, back_map)
    operands = [mine_now, modes, tab["decay"], tab["border_kappa"], tab["y_inv"], tab["z_inv"]]
    in_specs = [whole(mine_now.shape), pl.BlockSpec(block, ahead_map), whole(plane), whole(plane)]
    in_specs += [whole(tab["y_inv"].shape), whole(tab["z_inv"].shape)]
    if summed:
        operands += final
        in_specs += [pl.BlockSpec(memory_space=pltpu.SMEM)] + [behind] * 4
        out_shape = (field,) * 3
        out_specs = (behind,) * 3
    else:
        jumps = (2, size_x, size_z)
        out_shape = (field, shape_of(*plane), shape_of(*plane), shape_of(*jumps))
        out_specs = (behind, whole(plane), whole(plane), whole(jumps))
    voxels = float(devices * size_x * size_y * size_z)
    return pl.pallas_call(
        functools.partial(inverse_kernel, group, planes, summed, voxels, tab["mean_scale"]),
        grid=(2, blocks),
        out_shape=out_shape,
        in_specs=in_specs,
        out_specs=out_specs,
        scratch_shapes=[
            pltpu.VMEM(plane, F32),
            pltpu.VMEM((size_x,) + plane, F32),
            pltpu.VMEM((size_x,) + plane, F32),
            pltpu.VMEM((2, size_x, size_z), F32),
            pltpu.VMEM((2 * size_y, size_z), F32),
            pltpu.VMEM((size_z, size_x), F32),
            pltpu.VMEM((8, size_z), F32),
        ],
        compiler_params=params(2),
        name="inverse_modes",
    )(*operands)


def on_device(phase_ids, conduct_table, gradient, start_field):
    size_x, size_y, size_z = start_field.shape
    wide, narrow = lax.axis_size("wide"), lax.axis_size("narrow")
    tab = make_tables(size_x, size_y, size_z, wide, narrow)
    tab = {k: jnp.asarray(v) if isinstance(v, np.ndarray) and k != "sines" else v for k, v in tab.items()}
    group, planes = tab["group"], tab["planes"]
    blocks = size_x // planes
    plane = (size_y, size_z)
    block = (planes,) + plane
    wide_at, narrow_at = lax.axis_index("wide"), lax.axis_index("narrow")
    device = (wide_at * narrow + narrow_at).astype(jnp.int32)
    theta = lax.dynamic_index_in_dim(tab["theta"], device, 0, False)[:, :, None]
    along_x = jnp.arange(size_x, dtype=F32)
    tab["decay_powers"] = jnp.concatenate(
        [jnp.exp(-theta * along_x), jnp.exp(-theta * (size_x - 1.0 - along_x))], axis=1
    )
    device = device.reshape(1)
    flags = jnp.stack([wide_at > 0, wide_at < wide - 1, narrow_at > 0, narrow_at < narrow - 1])
    scal = jnp.concatenate([(0.5 / conduct_table).T.reshape(-1), gradient, flags.astype(F32)])
    kappa = tab["kappa"] / jnp.mean(conduct_table)

    edge = lambda dim, at: jnp.stack(
        [lax.index_in_dim(phase_ids, at, dim, False).astype(F32), lax.index_in_dim(start_field, at, dim, False)]
    )
    x_before, x_after = exchange(edge(0, 0), edge(0, size_x - 1), "wide")
    y_before, y_after = exchange(edge(1, 0), edge(1, size_y - 1), "narrow")

    main = pl.BlockSpec(block, lambda i: (i, 0, 0))
    following = pl.BlockSpec((1,) + plane, lambda i: (jnp.minimum((i + 1) * planes, size_x - 1), 0, 0))
    field_shape = shape_of(size_x, *plane)
    matrices = [whole(tab["z_fwd"].shape), whole(tab["y_fwd"].shape), whole(plane), whole(plane)]
    carried = [pltpu.VMEM(plane, F32), pltpu.VMEM(plane, F32)]
    residual, modes, fx, fy, fz, fx_low, fy_low, ahead, back = pl.pallas_call(
        functools.partial(residual_kernel, group, planes),
        grid=(blocks,),
        out_shape=(field_shape,) * 5 + (shape_of(*plane), shape_of(size_x, size_z)) + (shape_of(*plane),) * 2,
        in_specs=[pl.BlockSpec(memory_space=pltpu.SMEM), main, following, main, following]
        + [whole((2,) + plane)] * 2
        + [whole((2, size_x, size_z))] * 2
        + matrices,
        out_specs=(main,) * 5 + (whole(plane), whole((size_x, size_z))) + (whole(plane),) * 2,
        scratch_shapes=carried,
        compiler_params=params(1),
        name="residual_modes",
    )(
        scal, phase_ids, phase_ids, start_field, start_field, x_before, x_after, y_before, y_after,
        tab["z_fwd"], tab["y_fwd"], kappa, tab["decay"],
    )
    along, xb, xa, jumps = solve(modes, ahead, back, tab, device)

    image, modes, ahead, back, sums = pl.pallas_call(
        functools.partial(image_kernel, group, planes),
        grid=(blocks,),
        out_shape=(field_shape,) * 2 + (shape_of(*plane),) * 2 + (shape_of(5, 8, size_z),),
        in_specs=[main, following] + [main] * 4
        + [whole(plane), whole((size_x, size_z))]
        + [whole(plane)] * 2
        + [whole((2, size_x, size_z))]
        + matrices,
        out_specs=(main,) * 2 + (whole(plane),) * 2 + (whole((5, 8, size_z)),),
        scratch_shapes=carried,
        compiler_params=params(1),
        name="image_modes",
    )(
        along, along, residual, fx, fy, fz, fx_low, fy_low, xb, xa, jumps,
        tab["z_fwd"], tab["y_fwd"], kappa, tab["decay"],
    )
    base = jnp.mean(conduct_table).reshape(1)
    new_direction, result, residual_next = solve(
        modes, ahead, back, tab, device, sums, [base, residual, image, along, start_field]
    )
    return result, residual_next, new_direction


def solution(mesh):
    placed = (P("wide", "narrow", None), P(), P(), P("wide", "narrow", None))
    return jax.shard_map(
        on_device,
        mesh=mesh,
        in_specs=placed,
        out_specs=(P("wide", "narrow", None),) * 3,
        check_vma=False,
    )
```

```python
import functools

import jax
import jax.numpy as jnp
import ml_dtypes
import numpy as np
from jax import lax
from jax.experimental import pallas as pl
from jax.experimental.pallas import tpu as pltpu
from jax.sharding import PartitionSpec as P

PHASES = 4
F32 = jnp.float32
BF16 = jnp.bfloat16
VMEM_LIMIT = 56 * 1024 * 1024
PLANES = 32
FORWARD_TERMS = ((0, 0), (0, 1), (1, 0), (1, 1), (0, 2), (2, 0))
INVERSE_TERMS = ((0, 0), (0, 1), (1, 0))


def cosine_table(length):
    m = np.arange(length)[:, None]
    n = np.arange(length)[None, :]
    weight = np.where(m == 0, np.sqrt(1.0 / length), np.sqrt(2.0 / length))
    return weight * np.cos(np.pi * (m * (2 * n + 1) % (4 * length)) / (2.0 * length))


def eigen_values(length):
    return 4.0 * np.sin(np.pi * np.arange(length) / (2.0 * length)) ** 2


def pieces(matrix, count=3):
    rest = np.asarray(matrix, np.float64)
    result = []
    for _ in range(count):
        piece = rest.astype(np.float32).astype(ml_dtypes.bfloat16)
        result.append(piece)
        rest = rest - piece.astype(np.float64)
    return np.stack(result)


def make_tables(size_x, size_y, size_z, wide, narrow):
    length_x = size_x * wide
    group = min(max(256 // size_y, 1), size_x)
    parity = np.concatenate([np.arange(0, size_y, 2), np.arange(1, size_y, 2)])
    strip = cosine_table(size_y)[parity]
    block_y = np.kron(np.eye(group), strip)
    table_z = cosine_table(size_z)
    shift = 4.0 * np.sin(np.pi / (2.0 * length_x)) ** 2
    eig_z = eigen_values(size_z)
    sigma = shift + eigen_values(size_y)[parity][:, None] + eig_z[None, :]
    theta = 2.0 * np.arcsinh(np.sqrt(sigma) / 2.0)
    decay = np.exp(-theta)
    square_rest = -np.expm1(-2.0 * theta)
    step = np.exp(-theta * size_x)
    total = -np.expm1(-2.0 * wide * size_x * theta)
    powers = np.stack([step**t / total for t in range(2 * wide)])
    border = np.broadcast_to(strip[:, :1], sigma.shape)
    eta = 2.0 * np.arcsinh(
        np.sqrt(shift + eig_z[:, None] + eigen_values(length_x)[None, :]) / 2.0
    )
    fade = np.exp(-eta * size_y)
    half_angle = np.pi * np.arange(1, narrow) / (2.0 * narrow)
    capacity = (np.tanh(eta / 2.0) * -np.expm1(-2.0 * eta * size_y))[None] / (
        (np.expm1(-eta * size_y) ** 2)[None]
        + 4.0 * fade[None] * (np.sin(half_angle) ** 2)[:, None, None]
    )
    devices = wide * narrow
    part = size_z // devices
    capacity = capacity.reshape(narrow - 1, devices, part, length_x).transpose(1, 0, 2, 3)
    k = np.arange(1, narrow)
    sines = np.sqrt(2.0 / narrow) * np.sin(np.pi * k[:, None] * k[None, :] / narrow)
    table_x = cosine_table(length_x).T.reshape(wide, size_x, length_x)
    by_mode = lambda left, right: np.concatenate([left.T, right.T], axis=1).reshape(devices, part, 2 * size_y)
    mix = np.stack(
        [
            np.stack(
                [
                    np.stack(
                        [
                            by_mode(powers[(d - 1 - b) % (2 * wide)], powers[(b - 1 - d) % (2 * wide)]),
                            by_mode(powers[(d + b) % (2 * wide)], powers[(2 * wide - 2 - b - d) % (2 * wide)]),
                        ],
                        axis=1,
                    )
                    for b in range(wide)
                ],
                axis=1,
            )
            for d in range(wide)
        ],
        axis=1,
    )
    even = np.broadcast_to((np.arange(size_y) < (size_y + 1) // 2)[:, None], sigma.shape)
    end = border * decay
    row = end / square_rest
    twice = lambda values: by_mode(values, values)
    f32 = lambda a: np.asarray(a, np.float32)
    return dict(
        group=group,
        planes=min(PLANES, size_x),
        z_fwd=pieces(table_z.T),
        z_inv=pieces(table_z, 2),
        y_fwd=pieces(block_y),
        y_inv=pieces(block_y.T, 2),
        theta=f32(theta.T.reshape(devices, part, size_y)),
        decay=f32(decay),
        border=f32(border),
        border_decay=f32(end),
        mix=f32(mix),
        row_even=f32(twice(np.where(even, row, 0.0))),
        row_odd=f32(twice(np.where(even, 0.0, row))),
        row_dot=f32(twice(1.0 / square_rest)),
        decay_inverse=f32(1.0 / decay),
        rest_inverse=f32(1.0 / square_rest),
        rest=f32(-np.expm1(-theta)),
        decay_rest=f32(decay / square_rest),
        mean_scale=float(np.sqrt(size_y * size_z) / (shift * decay[0, 0])),
        shift=float(shift),
        end_even=f32(twice(np.where(even, end, 0.0))),
        end_odd=f32(twice(np.where(even, 0.0, end))),
        capacity=f32(capacity.reshape(devices, (narrow - 1) * part, length_x)),
        sines=sines,
        table_x=f32(table_x),
    )


def split(values, count):
    result = [values.astype(BF16)]
    rest = values
    for _ in range(count - 1):
        rest = rest - result[-1].astype(F32)
        result.append(rest.astype(BF16))
    return result


def product_right(values, matrix_ref, terms):
    parts = split(values, 1 + max(a for a, _ in terms))
    total = None
    for a, b in reversed(terms):
        term = jnp.dot(parts[a], matrix_ref[b], preferred_element_type=F32)
        total = term if total is None else total + term
    return total


def product_left(matrix_ref, values, terms):
    parts = split(values, 1 + max(a for a, _ in terms))
    total = None
    for a, b in reversed(terms):
        term = jnp.dot(matrix_ref[b], parts[a], preferred_element_type=F32)
        total = term if total is None else total + term
    return total


def lookup(phase, scal, component):
    base = 4 * component
    picked = jnp.where(phase == 2.0, scal[base + 2], scal[base + 3])
    picked = jnp.where(phase == 1.0, scal[base + 1], picked)
    return jnp.where(phase == 0.0, scal[base], picked)


def forward_modes(first, block, base_inverse, z_ref, y_ref, decay_ref, sweep_ref, ahead_ref, back_ref, corner_ref, power):
    rows = block[0].shape[0]
    flat = jnp.concatenate(block, axis=0)
    flat = product_right(flat, z_ref, FORWARD_TERMS)
    flat = product_left(y_ref, flat, FORWARD_TERMS)
    decay = decay_ref[...]
    scale = decay * base_inverse
    ahead, back, weight, corner = (ahead_ref[...], back_ref[...], power[...], corner_ref[...])
    for j in range(len(block)):
        scaled = flat[j * rows : (j + 1) * rows] * scale
        ahead = decay * ahead + scaled
        sweep_ref[first + j] = ahead
        back = back + weight * scaled
        weight = weight * decay
        corner = corner + scaled[:8, :128]
    ahead_ref[...] = ahead
    back_ref[...] = back
    power[...] = weight
    corner_ref[...] = corner


def fold(values):
    rows, depth = values.shape
    return jnp.sum(values.reshape(rows // 8, 8, depth), axis=0)


def residual_kernel(
    group, planes,
    scal, phase_ref, phase_next, field_ref, field_next, x_before, x_after, y_before, y_after,
    z_mat, y_mat, decay_ref,
    residual_ref, sweep_ref, fx_ref, fy_ref, fz_ref, fx_low, fy_low, ahead_ref, back_ref, corner_ref,
    flux_low, power,
):
    step = pl.program_id(0)
    rows, depth = flux_low.shape
    gx, gy, gz = scal[12], scal[13], scal[14]
    flag_xb, flag_xa, flag_yb, flag_ya = scal[15], scal[16], scal[17], scal[18]
    row = lax.broadcasted_iota(jnp.int32, (rows, depth), 0)
    lane = lax.broadcasted_iota(jnp.int32, (rows, depth), 1)

    @pl.when(step == 0)
    def _():
        face = flag_xb / (lookup(x_before[0], scal, 0) + lookup(phase_ref[0].astype(F32), scal, 0))
        fx_low[...] = face
        flux_low[...] = face * (field_ref[0] - x_before[1] + gx)
        ahead_ref[...] = jnp.zeros_like(ahead_ref)
        back_ref[...] = jnp.zeros_like(back_ref)
        corner_ref[...] = jnp.zeros_like(corner_ref)
        power[...] = jnp.ones_like(power)

    last = step == pl.num_programs(0) - 1
    end_phase = jnp.where(last, x_after[0], phase_next[0].astype(F32))
    end_field = jnp.where(last, x_after[1], field_next[0])
    flag_end = jnp.where(last, flag_xa, 1.0)
    flux_x_low = flux_low[...]
    hx = lookup(phase_ref[0].astype(F32), scal, 0)
    done = []
    for j in range(planes):
        x = step * planes + j
        phase = phase_ref[j].astype(F32)
        field = field_ref[j]
        if j + 1 < planes:
            hx_next = lookup(phase_ref[j + 1].astype(F32), scal, 0)
            field_up = field_ref[j + 1]
            fx = 1.0 / (hx + hx_next)
        else:
            hx_next = lookup(end_phase, scal, 0)
            field_up = end_field
            fx = flag_end / (hx + hx_next)
        flux_x = fx * (field_up - field + gx)
        total = flux_x - flux_x_low
        flux_x_low, hx = flux_x, hx_next
        fx_ref[j] = fx

        hy = lookup(phase, scal, 1)
        hy_up = jnp.where(
            row == rows - 1,
            lookup(y_after[0, pl.ds(x, 1), :], scal, 1),
            pltpu.roll(hy, rows - 1, 0),
        )
        fy = jnp.where(row == rows - 1, flag_ya, 1.0) / (hy + hy_up)
        v_up = jnp.where(row == rows - 1, y_after[1, pl.ds(x, 1), :], pltpu.roll(field, rows - 1, 0))
        flux_y = fy * (v_up - field + gy)
        face = flag_yb / (lookup(y_before[0, pl.ds(x, 1), :], scal, 1) + hy[0:1])
        low = face * (field[0:1] - y_before[1, pl.ds(x, 1), :] + gy)
        total = total + (flux_y - jnp.where(row == 0, low, pltpu.roll(flux_y, 1, 0)))
        fy_ref[j] = fy
        fy_low[pl.ds(x, 1), :] = face

        hz = lookup(phase, scal, 2)
        fz = jnp.where(lane == depth - 1, 0.0, 1.0 / (hz + pltpu.roll(hz, depth - 1, 1)))
        flux_z = fz * (pltpu.roll(field, depth - 1, 1) - field + gz)
        total = total + (flux_z - pltpu.roll(flux_z, 1, 1))
        fz_ref[j] = fz
        residual_ref[j] = total
        done.append(total)
        if len(done) == group:
            forward_modes(
                j + 1 - group, done, scal[19], z_mat, y_mat, decay_ref, sweep_ref, ahead_ref, back_ref, corner_ref, power
            )
            done = []
    flux_low[...] = flux_x_low


def image_kernel(
    group, planes,
    scal, field_ref, field_next, fx_ref, fy_ref, fz_ref, fx_low, fy_low,
    x_jump, y_jump, z_mat, y_mat, decay_ref,
    image_ref, sweep_ref, ahead_ref, back_ref, corner_ref, sums_ref,
    flux_low, power,
):
    step = pl.program_id(0)
    rows, depth = flux_low.shape
    row = lax.broadcasted_iota(jnp.int32, (rows, depth), 0)

    @pl.when(step == 0)
    def _():
        flux_low[...] = fx_low[...] * x_jump[0]
        ahead_ref[...] = jnp.zeros_like(ahead_ref)
        back_ref[...] = jnp.zeros_like(back_ref)
        corner_ref[...] = jnp.zeros_like(corner_ref)
        power[...] = jnp.ones_like(power)
        sums_ref[...] = jnp.zeros_like(sums_ref)

    last = step == pl.num_programs(0) - 1
    end_jump = jnp.where(last, x_jump[1], field_next[0] - field_ref[planes - 1])
    flux_x_low = flux_low[...]
    sums = sums_ref[...]
    done = []
    for j in range(planes):
        x = step * planes + j
        field = field_ref[j]
        flux_x = fx_ref[j] * (field_ref[j + 1] - field if j + 1 < planes else end_jump)
        total = flux_x_low - flux_x
        flux_x_low = flux_x
        jump = jnp.where(row == rows - 1, y_jump[1, pl.ds(x, 1), :], pltpu.roll(field, rows - 1, 0) - field)
        flux_y = fy_ref[j] * jump
        low = fy_low[pl.ds(x, 1), :] * y_jump[0, pl.ds(x, 1), :]
        total = total + (jnp.where(row == 0, low, pltpu.roll(flux_y, 1, 0)) - flux_y)
        flux_z = fz_ref[j] * (pltpu.roll(field, depth - 1, 1) - field)
        total = total + (pltpu.roll(flux_z, 1, 1) - flux_z)
        image_ref[j] = total
        sums = sums + fold(field * total)
        done.append(total)
        if len(done) == group:
            forward_modes(
                j + 1 - group, done, scal[19], z_mat, y_mat, decay_ref, sweep_ref, ahead_ref, back_ref, corner_ref, power
            )
            done = []
    sums_ref[...] = sums
    flux_low[...] = flux_x_low


def local_kernel(
    devices, planes, summed,
    sweep_ref, ahead_ref, back_ref, corner_ref, decay_ref, border_ref, decay_inverse, decay_rest, *rest,
):
    if summed:
        sums_ref, earlier_ref, share_ref = rest[:3]
    out_ref, facts_ref, run, dots, rows_ref = rest[-5:]
    step = pl.program_id(0)
    blocks = pl.num_programs(0)
    decay = decay_ref[...]
    border = border_ref[...]
    half = decay.shape[0] // 2

    @pl.when(step == 0)
    def _():
        run[...] = ahead_ref[...] * decay_rest[...]
        dots[...] = jnp.zeros_like(dots)

    value, total = run[...], dots[...]
    first = (blocks - 1 - step) * planes
    for j in reversed(range(planes)):
        swept = sweep_ref[j]
        total = total + swept * swept
        value = swept + decay * value
        mode = value * border
        rows_ref[0, pl.ds(first + j, 1), :] = jnp.sum(mode[:half], axis=0, keepdims=True)
        rows_ref[1, pl.ds(first + j, 1), :] = jnp.sum(mode[half:], axis=0, keepdims=True)
    run[...] = value
    dots[...] = total

    @pl.when(step == blocks - 1)
    def _():
        part, width = out_ref.shape[2:]
        ahead = ahead_ref[...]
        ends = jnp.concatenate([ahead, back_ref[...]], axis=0)
        for slot, turned in enumerate((rows_ref[0].T, rows_ref[1].T, ends.T)):
            for j in range(devices):
                out_ref[j, slot] = turned[j * part : (j + 1) * part]
        lane = lax.broadcasted_iota(jnp.int32, facts_ref.shape, 1)
        square = jnp.sum(total * decay_inverse[...] + ahead * ahead * decay_rest[...])
        facts = jnp.where(lane == 0, square, 0.0) + jnp.where(lane == 1, jnp.sum(corner_ref[:1, :1]), 0.0)
        if summed:
            facts = facts + jnp.where(lane == 4, jnp.sum(sums_ref[...]), 0.0)
            facts = facts + pltpu.roll(earlier_ref[...] + share_ref[...], 2, 1)
        facts_ref[...] = facts


def faces_kernel(
    wide, narrow, part, sines, summed,
    device, got_ref, table_ref, capacity_ref, power_ref, mix_ref, row_even, row_odd, end_even, end_odd, row_dot,
    *rest,
):
    if summed:
        facts_ref, out_ref, jumps, modes = rest
    else:
        out_ref, share_ref, jumps, modes = rest
    devices = wide * narrow
    width = got_ref.shape[1]
    slots = 3
    out_slots = 4 if summed else 3
    faces = narrow - 1
    highest = dict(preferred_element_type=F32, precision=lax.Precision.HIGHEST)

    def take(ref, slot, mode, count):
        return ref[pl.ds(slot * part + mode, devices, stride=count * part), :]

    def incoming(ends, mode):
        swapped = pltpu.roll(ends, width // 2, 1)
        result = []
        for mine in range(wide):
            total = None
            for block in range(wide):
                at = slice(block * narrow, (block + 1) * narrow)
                term = mix_ref[0, mine, block, 0, pl.ds(mode, 1), :] * ends[at]
                term = term + mix_ref[0, mine, block, 1, pl.ds(mode, 1), :] * swapped[at]
                total = term if total is None else total + term
            result.append(total)
        return jnp.concatenate(result, axis=0)

    inner = None
    for mode in range(part):
        ends = take(got_ref, 2, mode, slots)
        entering = incoming(ends, mode)
        term = entering * pltpu.roll(ends, width // 2, 1) * row_dot[0, pl.ds(mode, 1), :]
        inner = term if inner is None else inner + term
        both = jnp.concatenate(
            [entering * row_even[0, pl.ds(mode, 1), :], entering * row_odd[0, pl.ds(mode, 1), :]], axis=0
        )
        added = jnp.dot(both, power_ref[mode], **highest)
        even = take(got_ref, 0, mode, slots) + added[:devices]
        odd = take(got_ref, 1, mode, slots) + added[devices:]
        jump = pltpu.roll(even + odd, devices - 1, 0) - (even - odd)
        jumps[pl.ds(mode, devices, stride=part), :] = jump
    mixed = None
    for block in range(wide):
        strips = [jumps[pl.ds((block * narrow + i) * part, part), :] for i in range(faces)]
        for k in range(faces):
            acc = None
            for i in range(faces):
                term = strips[i] * float(sines[k, i])
                acc = term if acc is None else acc + term
            modes[pl.ds(k * part, part), :] = acc
        term = jnp.dot(modes[...], table_ref[block], **highest)
        mixed = term if mixed is None else mixed + term
    plain = mixed
    mixed = mixed * capacity_ref[0]
    for block in range(wide):
        modes[...] = lax.dot_general(mixed, table_ref[block], (((1,), (1,)), ((), ())), **highest)
        solved = []
        for k in range(faces):
            acc = None
            for i in range(faces):
                term = modes[pl.ds(i * part, part), :] * float(sines[k, i])
                acc = term if acc is None else acc + term
            solved.append(acc)
        for strip in range(narrow):
            below = solved[strip - 1] if strip > 0 else jnp.zeros_like(solved[0])
            above = solved[strip] if strip < faces else jnp.zeros_like(solved[0])
            at = (block * narrow + strip) * out_slots * part
            out_ref[pl.ds(at, part), :] = above - below
            out_ref[pl.ds(at + part, part), :] = -(above + below)
    for mode in range(part):
        both = jnp.concatenate([take(out_ref, 0, mode, out_slots), take(out_ref, 1, mode, out_slots)], axis=0)
        added = lax.dot_general(both, power_ref[mode], (((1,), (1,)), ((), ())), **highest)
        added = pltpu.roll(added, width // 2, 1)
        ends = take(got_ref, 2, mode, slots) + end_even[0, pl.ds(mode, 1), :] * added[:devices]
        ends = ends + end_odd[0, pl.ds(mode, 1), :] * added[devices:]
        out_ref[pl.ds(2 * part + mode, devices, stride=out_slots * part), :] = incoming(ends, mode)
    share = jnp.sum(inner) - jnp.sum(plain * mixed)
    if summed:
        lane = lax.broadcasted_iota(jnp.int32, (part, width), 1)
        facts = facts_ref[:1, :width] + jnp.where(lane == 0, share, 0.0)
        for j in range(devices):
            out_ref[pl.ds((j * out_slots + 3) * part, part), :] = facts
    else:
        lane = lax.broadcasted_iota(jnp.int32, share_ref.shape, 1)
        share_ref[...] = jnp.where(lane == 0, share, 0.0)


def inverse_kernel(
    group, planes, dotted, voxels, mean_scale, shift,
    scal, faces_ref, sweep_ref, decay_ref, scale_ref, rest_inverse, decay_rest, rest_ref, y_mat, z_mat, *rest,
):
    if dotted:
        residual_ref, image_ref, along_ref, start_ref = rest[:4]
        out_ref, solution_ref, next_ref = rest[4:7]
    else:
        out_ref, jump_x, jump_y = rest[:3]
    run, added, rows_ref, entering, turned, factors = rest[-6:]
    step = pl.program_id(0)
    blocks = pl.num_programs(0)
    decay = decay_ref[...]
    rows, depth = decay.shape
    half = rows // 2

    @pl.when(step == 0)
    def _():
        devices, _, part, _ = faces_ref.shape
        for slot in range(3):
            for j in range(devices):
                turned[pl.ds(j * part, part), :] = faces_ref[j, slot]
            if slot < 2:
                rows_ref[slot] = turned[...].T
            else:
                entering[...] = turned[...].T
        scale = scale_ref[...]

        def body(x, value):
            face = jnp.concatenate(
                [
                    jnp.broadcast_to(rows_ref[0, pl.ds(x, 1), :], (half, depth)),
                    jnp.broadcast_to(rows_ref[1, pl.ds(x, 1), :], (half, depth)),
                ],
                axis=0,
            )
            value = decay * value + scale * face
            added[x] = value
            return value

        value = lax.fori_loop(0, blocks * planes, body, entering[pl.ds(0, rows), :], unroll=8)
        value = value + sweep_ref[planes - 1]
        beyond = decay_rest[...] * value + rest_inverse[...] * entering[pl.ds(rows, rows), :]
        run[...] = beyond
        if not dotted:
            entering[pl.ds(rows, rows), :] = rest_ref[...] * beyond - value

        if dotted:
            total = faces_ref[0, 3]
            for j in range(1, devices):
                total = total + faces_ref[j, 3]
            total = total[:1]
            lane = lax.broadcasted_iota(jnp.int32, total.shape, 1)
            pick = lambda i: jnp.sum(jnp.where(lane == i, total, 0.0), axis=1, keepdims=True)
            base = scal[20]

            def solved(square, constant):
                mean = constant * (mean_scale / voxels)
                field = constant * base * (mean_scale * shift)
                return mean, field, base * square - mean * field

            mean, image_sum, square = solved(pick(0), pick(1))
            mean_along, _, rz_now = solved(pick(2), pick(3))
            alpha = rz_now / (pick(4) - mean_along * image_sum)
            ratio = alpha * (alpha * square) / rz_now
            for i, factor in enumerate((alpha, mean_along, ratio, ratio * mean_along - alpha * mean)):
                factors[pl.ds(i, 1), :] = jnp.broadcast_to(factor, (1, depth))

    value = run[...]
    first = (blocks - 1 - step) * planes
    if dotted:
        alpha, mean, ratio, offset = [
            jnp.broadcast_to(factors[pl.ds(i, 1), :], (rows, depth)) for i in range(4)
        ]
    for start in reversed(range(0, planes, group)):
        modes = [None] * group
        for j in reversed(range(group)):
            value = (sweep_ref[start + j] + added[first + start + j]) + decay * value
            modes[j] = value
        flat = jnp.concatenate(modes, axis=0)
        flat = product_left(y_mat, flat, INVERSE_TERMS)
        flat = product_right(flat, z_mat, INVERSE_TERMS)
        for j in range(group):
            at = start + j
            plane = flat[j * rows : (j + 1) * rows]
            if dotted:
                along = along_ref[at]
                next_ref[at] = residual_ref[at] - alpha * image_ref[at]
                solution_ref[at] = start_ref[at] + alpha * (along - mean)
                plane = (ratio * along - offset) - alpha * plane
            out_ref[at] = plane
    run[...] = value

    if not dotted:
        @pl.when(step == blocks - 1)
        def _():
            before = rest_ref[...] * run[...] - entering[pl.ds(0, rows), :]
            flat = jnp.concatenate([before, entering[pl.ds(rows, rows), :]] * (group // 2), axis=0)
            flat = product_left(y_mat, flat, INVERSE_TERMS)
            flat = product_right(flat, z_mat, INVERSE_TERMS)
            jump_x[0] = flat[:rows]
            jump_x[1] = flat[rows : 2 * rows]
            jump_y[0] = product_right(-0.5 * (rows_ref[0] + rows_ref[1]), z_mat, INVERSE_TERMS)
            jump_y[1] = product_right(0.5 * (rows_ref[0] - rows_ref[1]), z_mat, INVERSE_TERMS)


def whole(shape, single=False):
    mode = dict(pipeline_mode=pl.Buffered(1)) if single else {}
    return pl.BlockSpec(shape, lambda *_: (0,) * len(shape), **mode)


def shape_of(*dims):
    return jax.ShapeDtypeStruct(dims, F32)


def params(dims):
    return pltpu.CompilerParams(dimension_semantics=("arbitrary",) * dims, vmem_limit_bytes=VMEM_LIMIT)


def neighbours(axis):
    devices = lax.axis_size(axis)
    up = [(i, i + 1) for i in range(devices - 1)]
    return up, [(j, i) for i, j in up]


def exchange(first, last, axis):
    up, down = neighbours(axis)
    return lax.ppermute(last, axis, up), lax.ppermute(first, axis, down)


def solve(forward, tab, device, scal, earlier=(), final=()):
    sweep, ahead, back, corner = forward
    size_x, size_y, size_z = sweep.shape
    wide, narrow = lax.axis_size("wide"), lax.axis_size("narrow")
    devices = wide * narrow
    group, planes = tab["group"], tab["planes"]
    blocks = size_x // planes
    part = size_z // devices
    plane = (size_y, size_z)
    block = (planes,) + plane
    summed = bool(final)
    field = shape_of(size_x, *plane)
    behind = pl.BlockSpec(block, lambda i: (blocks - 1 - i, 0, 0))
    packed = (devices, 3, part, size_x)
    sent, facts = pl.pallas_call(
        functools.partial(local_kernel, devices, planes, summed),
        grid=(blocks,),
        out_shape=(shape_of(*packed), shape_of(8, 128)),
        in_specs=[behind]
        + [whole(plane)] * 2
        + [whole((8, 128))]
        + [whole(plane)] * 4
        + [whole((8, size_z)), whole((8, 128)), whole((8, 128))] * summed,
        out_specs=(whole(packed), whole((8, 128))),
        scratch_shapes=[pltpu.VMEM(plane, F32), pltpu.VMEM(plane, F32), pltpu.VMEM((2, size_x, size_z), F32)],
        compiler_params=params(1),
        name="strip_borders",
    )(
        sweep, ahead, back, corner, tab["decay"], tab["border"], tab["decay_inverse"], tab["decay_rest"],
        *earlier,
    )
    got = lax.all_to_all(sent, ("wide", "narrow"), split_axis=0, concat_axis=0, tiled=True)
    faces = narrow - 1
    length_x = wide * size_x
    flat = (devices * 3 * part, size_x)
    out_slots = 4 if summed else 3
    flat_out = (devices * out_slots * part, size_x)
    small = (whole((8, 128)),)
    mine = lambda shape: pl.BlockSpec((1,) + shape, lambda i, idx: (idx[0],) + (0,) * len(shape))
    solved, *share = pl.pallas_call(
        functools.partial(faces_kernel, wide, narrow, part, tab["sines"], summed),
        out_shape=(shape_of(*flat_out),) + (shape_of(8, 128),) * (not summed),
        grid_spec=pltpu.PrefetchScalarGridSpec(
            num_scalar_prefetch=1,
            grid=(1,),
            in_specs=[
                whole(flat),
                whole((wide, size_x, length_x)),
                mine((faces * part, length_x)),
                whole((part, 2 * size_y, size_x)),
                mine((wide, wide, 2, part, size_x)),
            ]
            + [mine((part, size_x))] * 5
            + list(small) * summed,
            out_specs=(whole(flat_out),) + small * (not summed),
            scratch_shapes=[
                pltpu.VMEM((devices * part, size_x), F32),
                pltpu.VMEM((faces * part, size_x), F32),
            ],
        ),
        compiler_params=params(1),
        name="strip_faces",
    )(
        device, got.reshape(flat), tab["table_x"], tab["capacity"], tab["decay_powers"], tab["mix"],
        tab["row_even"], tab["row_odd"], tab["end_even"], tab["end_odd"], tab["row_dot"],
        *([facts] if summed else []),
    )
    mine_now = lax.all_to_all(
        solved.reshape(devices, out_slots, part, size_x), ("wide", "narrow"), split_axis=0, concat_axis=0, tiled=True
    )
    operands = [
        scal, mine_now, sweep, tab["decay"], tab["border_decay"], tab["rest_inverse"], tab["decay_rest"],
        tab["rest"], tab["y_inv"], tab["z_inv"],
    ]
    smem = pl.BlockSpec(memory_space=pltpu.SMEM)
    in_specs = [smem, whole(mine_now.shape), behind] + [whole(plane)] * 5
    in_specs += [whole(tab["y_inv"].shape), whole(tab["z_inv"].shape)]
    if summed:
        operands += final
        in_specs += [behind] * 4
        out_shape = (field,) * 3
        out_specs = (behind,) * 3
    else:
        jumps = (2, size_x, size_z)
        out_shape = (field, shape_of(2, *plane), shape_of(*jumps))
        out_specs = (behind, whole((2,) + plane), whole(jumps))
    voxels = float(devices * size_x * size_y * size_z)
    result = pl.pallas_call(
        functools.partial(inverse_kernel, group, planes, summed, voxels, tab["mean_scale"], tab["shift"]),
        grid=(blocks,),
        out_shape=out_shape,
        in_specs=in_specs,
        out_specs=out_specs,
        scratch_shapes=[
            pltpu.VMEM(plane, F32),
            pltpu.VMEM((size_x,) + plane, F32),
            pltpu.VMEM((2, size_x, size_z), F32),
            pltpu.VMEM((2 * size_y, size_z), F32),
            pltpu.VMEM((size_z, size_x), F32),
            pltpu.VMEM((8, size_z), F32),
        ],
        compiler_params=params(1),
        name="inverse_modes",
    )(*operands)
    return result, [facts, *share]


def on_device(phase_ids, conduct_table, gradient, start_field):
    size_x, size_y, size_z = start_field.shape
    wide, narrow = lax.axis_size("wide"), lax.axis_size("narrow")
    tab = make_tables(size_x, size_y, size_z, wide, narrow)
    tab = {k: jnp.asarray(v) if isinstance(v, np.ndarray) and k != "sines" else v for k, v in tab.items()}
    group, planes = tab["group"], tab["planes"]
    blocks = size_x // planes
    plane = (size_y, size_z)
    block = (planes,) + plane
    wide_at, narrow_at = lax.axis_index("wide"), lax.axis_index("narrow")
    device = (wide_at * narrow + narrow_at).astype(jnp.int32)
    theta = lax.dynamic_index_in_dim(tab["theta"], device, 0, False)[:, :, None]
    along_x = jnp.arange(size_x, dtype=F32)
    tab["decay_powers"] = jnp.concatenate(
        [jnp.exp(-theta * along_x), jnp.exp(-theta * (size_x - 1.0 - along_x))], axis=1
    )
    device = device.reshape(1)
    flags = jnp.stack([wide_at > 0, wide_at < wide - 1, narrow_at > 0, narrow_at < narrow - 1])
    base = jnp.mean(conduct_table).reshape(1)
    scal = jnp.concatenate([(0.5 / conduct_table).T.reshape(-1), gradient, flags.astype(F32), 1.0 / base, base])
    scal, tab["decay_powers"], device = lax.optimization_barrier((scal, tab["decay_powers"], device))

    edge = lambda dim, at: jnp.stack(
        [lax.index_in_dim(phase_ids, at, dim, False).astype(F32), lax.index_in_dim(start_field, at, dim, False)]
    )
    x_before, x_after = exchange(edge(0, 0), edge(0, size_x - 1), "wide")
    y_before, y_after = exchange(edge(1, 0), edge(1, size_y - 1), "narrow")

    main = pl.BlockSpec(block, lambda i: (i, 0, 0))
    following = pl.BlockSpec((1,) + plane, lambda i: (jnp.minimum((i + 1) * planes, size_x - 1), 0, 0))
    field_shape = shape_of(size_x, *plane)
    end_shapes = (shape_of(*plane),) * 2 + (shape_of(8, 128),)
    end_specs = (whole(plane),) * 2 + (whole((8, 128)),)
    matrices = [whole(tab["z_fwd"].shape), whole(tab["y_fwd"].shape), whole(plane)]
    carried = [pltpu.VMEM(plane, F32), pltpu.VMEM(plane, F32)]
    residual, sweep, fx, fy, fz, fx_low, fy_low, *ends = pl.pallas_call(
        functools.partial(residual_kernel, group, planes),
        grid=(blocks,),
        out_shape=(field_shape,) * 5 + (shape_of(*plane), shape_of(size_x, size_z)) + end_shapes,
        in_specs=[pl.BlockSpec(memory_space=pltpu.SMEM), main, following, main, following]
        + [whole((2,) + plane)] * 2
        + [whole((2, size_x, size_z))] * 2
        + matrices,
        out_specs=(main,) * 5 + (whole(plane), whole((size_x, size_z))) + end_specs,
        scratch_shapes=carried,
        compiler_params=params(1),
        name="residual_modes",
    )(
        scal, phase_ids, phase_ids, start_field, start_field, x_before, x_after, y_before, y_after,
        tab["z_fwd"], tab["y_fwd"], tab["decay"],
    )
    (along, jump_x, jump_y), earlier = solve((sweep, *ends), tab, device, scal)

    image, sweep, *ends, sums = pl.pallas_call(
        functools.partial(image_kernel, group, planes),
        grid=(blocks,),
        out_shape=(field_shape,) * 2 + end_shapes + (shape_of(8, size_z),),
        in_specs=[pl.BlockSpec(memory_space=pltpu.SMEM), main, following] + [main] * 3
        + [whole(plane), whole((size_x, size_z))]
        + [whole((2,) + plane), whole((2, size_x, size_z))]
        + matrices,
        out_specs=(main,) * 2 + end_specs + (whole((8, size_z)),),
        scratch_shapes=carried,
        compiler_params=params(1),
        name="image_modes",
    )(
        scal, along, along, fx, fy, fz, fx_low, fy_low, jump_x, jump_y,
        tab["z_fwd"], tab["y_fwd"], tab["decay"],
    )
    (new_direction, result, residual_next), _ = solve(
        (sweep, *ends), tab, device, scal, [sums, *earlier], [residual, image, along, start_field]
    )
    return result, residual_next, new_direction


def solution(mesh):
    placed = (P("wide", "narrow", None), P(), P(), P("wide", "narrow", None))
    return jax.shard_map(
        on_device,
        mesh=mesh,
        in_specs=placed,
        out_specs=(P("wide", "narrow", None),) * 3,
        check_vma=False,
    )
```

```python
import functools

import jax
import jax.numpy as jnp
import ml_dtypes
import numpy as np
from jax import lax
from jax.experimental import pallas as pl
from jax.experimental.pallas import tpu as pltpu
from jax.sharding import PartitionSpec as P

PHASES = 4
F32 = jnp.float32
BF16 = jnp.bfloat16
VMEM_LIMIT = 56 * 1024 * 1024
PLANES = 32
FULL_TERMS = ((0, 0), (0, 1), (1, 0), (1, 1), (0, 2), (2, 0))
SHORT_TERMS = ((0, 0), (0, 1), (1, 0))


def cosine_table(length):
    m = np.arange(length)[:, None]
    n = np.arange(length)[None, :]
    weight = np.where(m == 0, np.sqrt(1.0 / length), np.sqrt(2.0 / length))
    return weight * np.cos(np.pi * (m * (2 * n + 1) % (4 * length)) / (2.0 * length))


def eigen_values(length):
    return 4.0 * np.sin(np.pi * np.arange(length) / (2.0 * length)) ** 2


def pieces(matrix, count=3):
    rest = np.asarray(matrix, np.float64)
    result = []
    for _ in range(count):
        piece = rest.astype(np.float32).astype(ml_dtypes.bfloat16)
        result.append(piece)
        rest = rest - piece.astype(np.float64)
    return np.stack(result)


def make_tables(size_x, size_y, size_z, wide, narrow):
    length_x = size_x * wide
    group = min(max(256 // size_y, 1), size_x)
    parity = np.concatenate([np.arange(0, size_y, 2), np.arange(1, size_y, 2)])
    strip = cosine_table(size_y)[parity]
    block_y = np.kron(np.eye(group), strip)
    table_z = cosine_table(size_z)
    shift = 4.0 * np.sin(np.pi / (2.0 * length_x)) ** 2
    eig_z = eigen_values(size_z)
    sigma = shift + eigen_values(size_y)[parity][:, None] + eig_z[None, :]
    theta = 2.0 * np.arcsinh(np.sqrt(sigma) / 2.0)
    decay = np.exp(-theta)
    square_rest = -np.expm1(-2.0 * theta)
    step = np.exp(-theta * size_x)
    total = -np.expm1(-2.0 * wide * size_x * theta)
    powers = np.stack([step**t / total for t in range(2 * wide)])
    border = np.broadcast_to(strip[:, :1], sigma.shape)
    eta = 2.0 * np.arcsinh(
        np.sqrt(shift + eig_z[:, None] + eigen_values(length_x)[None, :]) / 2.0
    )
    fade = np.exp(-eta * size_y)
    half_angle = np.pi * np.arange(1, narrow) / (2.0 * narrow)
    capacity = (np.tanh(eta / 2.0) * -np.expm1(-2.0 * eta * size_y))[None] / (
        (np.expm1(-eta * size_y) ** 2)[None]
        + 4.0 * fade[None] * (np.sin(half_angle) ** 2)[:, None, None]
    )
    devices = wide * narrow
    part = size_z // devices
    capacity = capacity.reshape(narrow - 1, devices, part, length_x).transpose(1, 0, 2, 3)
    k = np.arange(1, narrow)
    sines = np.sqrt(2.0 / narrow) * np.sin(np.pi * k[:, None] * k[None, :] / narrow)
    table_x = cosine_table(length_x).T.reshape(wide, size_x, length_x)
    by_mode = lambda left, right: np.concatenate([left.T, right.T], axis=1).reshape(devices, part, 2 * size_y)
    mix = np.stack(
        [
            np.stack(
                [
                    np.stack(
                        [
                            by_mode(powers[(d - 1 - b) % (2 * wide)], powers[(b - 1 - d) % (2 * wide)]),
                            by_mode(powers[(d + b) % (2 * wide)], powers[(2 * wide - 2 - b - d) % (2 * wide)]),
                        ],
                        axis=1,
                    )
                    for b in range(wide)
                ],
                axis=1,
            )
            for d in range(wide)
        ],
        axis=1,
    )
    even = np.broadcast_to((np.arange(size_y) < (size_y + 1) // 2)[:, None], sigma.shape)
    end = border * decay
    row = end / square_rest
    twice = lambda values: by_mode(values, values)
    f32 = lambda a: np.asarray(a, np.float32)
    return dict(
        group=group,
        planes=min(PLANES, size_x),
        z_fwd=pieces(table_z.T, 2),
        z_inv=pieces(table_z),
        y_fwd=pieces(block_y, 2),
        y_inv=pieces(block_y.T),
        theta=f32(theta.T.reshape(devices, part, size_y)),
        decay=f32(decay),
        border=f32(border),
        border_decay=f32(end),
        mix=f32(mix),
        row_even=f32(twice(np.where(even, row, 0.0))),
        row_odd=f32(twice(np.where(even, 0.0, row))),
        row_dot=f32(twice(1.0 / square_rest)),
        decay_inverse=f32(1.0 / decay),
        rest_inverse=f32(1.0 / square_rest),
        rest=f32(-np.expm1(-theta)),
        decay_rest=f32(decay / square_rest),
        mean_scale=float(np.sqrt(size_y * size_z) / (shift * decay[0, 0])),
        shift=float(shift),
        end_even=f32(twice(np.where(even, end, 0.0))),
        end_odd=f32(twice(np.where(even, 0.0, end))),
        capacity=f32(capacity.reshape(devices, (narrow - 1) * part, length_x)),
        sines=sines,
        table_x=f32(table_x),
    )


def split(values, count):
    result = [values.astype(BF16)]
    rest = values
    for _ in range(count - 1):
        rest = rest - result[-1].astype(F32)
        result.append(rest.astype(BF16))
    return result


def product_right(values, matrix_ref, terms):
    parts = split(values, 1 + max(a for a, _ in terms))
    total = None
    for a, b in reversed(terms):
        term = jnp.dot(parts[a], matrix_ref[b], preferred_element_type=F32)
        total = term if total is None else total + term
    return total


def product_left(matrix_ref, values, terms):
    parts = split(values, 1 + max(a for a, _ in terms))
    total = None
    for a, b in reversed(terms):
        term = jnp.dot(matrix_ref[b], parts[a], preferred_element_type=F32)
        total = term if total is None else total + term
    return total


def lookup(phase, scal, component):
    base = 4 * component
    picked = jnp.where(phase == 2.0, scal[base + 2], scal[base + 3])
    picked = jnp.where(phase == 1.0, scal[base + 1], picked)
    return jnp.where(phase == 0.0, scal[base], picked)


def forward_modes(first, block, base_inverse, z_ref, y_ref, decay_ref, sweep_ref, ahead_ref, back_ref, corner_ref, power):
    rows = block[0].shape[0]
    flat = jnp.concatenate(block, axis=0)
    flat = product_right(flat, z_ref, SHORT_TERMS)
    flat = product_left(y_ref, flat, SHORT_TERMS)
    decay = decay_ref[...]
    scale = decay * base_inverse
    ahead, back, weight, corner = (ahead_ref[...], back_ref[...], power[...], corner_ref[...])
    for j in range(len(block)):
        scaled = flat[j * rows : (j + 1) * rows] * scale
        ahead = decay * ahead + scaled
        sweep_ref[first + j] = ahead
        back = back + weight * scaled
        weight = weight * decay
        corner = corner + scaled[:8, :128]
    ahead_ref[...] = ahead
    back_ref[...] = back
    power[...] = weight
    corner_ref[...] = corner


def fold(values):
    rows, depth = values.shape
    return jnp.sum(values.reshape(rows // 8, 8, depth), axis=0)


def residual_kernel(
    group, planes,
    scal, phase_ref, phase_next, field_ref, field_next, x_before, x_after, y_before, y_after,
    z_mat, y_mat, decay_ref,
    residual_ref, sweep_ref, fx_ref, fy_ref, fz_ref, fx_low, fy_low, ahead_ref, back_ref, corner_ref,
    flux_low, power,
):
    step = pl.program_id(0)
    rows, depth = flux_low.shape
    gx, gy, gz = scal[12], scal[13], scal[14]
    flag_xb, flag_xa, flag_yb, flag_ya = scal[15], scal[16], scal[17], scal[18]
    row = lax.broadcasted_iota(jnp.int32, (rows, depth), 0)
    lane = lax.broadcasted_iota(jnp.int32, (rows, depth), 1)

    @pl.when(step == 0)
    def _():
        face = flag_xb / (lookup(x_before[0], scal, 0) + lookup(phase_ref[0].astype(F32), scal, 0))
        fx_low[...] = face
        flux_low[...] = face * (field_ref[0] - x_before[1] + gx)
        ahead_ref[...] = jnp.zeros_like(ahead_ref)
        back_ref[...] = jnp.zeros_like(back_ref)
        corner_ref[...] = jnp.zeros_like(corner_ref)
        power[...] = jnp.ones_like(power)

    last = step == pl.num_programs(0) - 1
    end_phase = jnp.where(last, x_after[0], phase_next[0].astype(F32))
    end_field = jnp.where(last, x_after[1], field_next[0])
    flag_end = jnp.where(last, flag_xa, 1.0)
    flux_x_low = flux_low[...]
    hx = lookup(phase_ref[0].astype(F32), scal, 0)
    done = []
    for j in range(planes):
        x = step * planes + j
        phase = phase_ref[j].astype(F32)
        field = field_ref[j]
        if j + 1 < planes:
            hx_next = lookup(phase_ref[j + 1].astype(F32), scal, 0)
            field_up = field_ref[j + 1]
            fx = 1.0 / (hx + hx_next)
        else:
            hx_next = lookup(end_phase, scal, 0)
            field_up = end_field
            fx = flag_end / (hx + hx_next)
        flux_x = fx * (field_up - field + gx)
        total = flux_x - flux_x_low
        flux_x_low, hx = flux_x, hx_next
        fx_ref[j] = fx

        hy = lookup(phase, scal, 1)
        hy_up = jnp.where(
            row == rows - 1,
            lookup(y_after[0, pl.ds(x, 1), :], scal, 1),
            pltpu.roll(hy, rows - 1, 0),
        )
        fy = jnp.where(row == rows - 1, flag_ya, 1.0) / (hy + hy_up)
        v_up = jnp.where(row == rows - 1, y_after[1, pl.ds(x, 1), :], pltpu.roll(field, rows - 1, 0))
        flux_y = fy * (v_up - field + gy)
        face = flag_yb / (lookup(y_before[0, pl.ds(x, 1), :], scal, 1) + hy[0:1])
        low = face * (field[0:1] - y_before[1, pl.ds(x, 1), :] + gy)
        total = total + (flux_y - jnp.where(row == 0, low, pltpu.roll(flux_y, 1, 0)))
        fy_ref[j] = fy
        fy_low[pl.ds(x, 1), :] = face

        hz = lookup(phase, scal, 2)
        fz = jnp.where(lane == depth - 1, 0.0, 1.0 / (hz + pltpu.roll(hz, depth - 1, 1)))
        flux_z = fz * (pltpu.roll(field, depth - 1, 1) - field + gz)
        total = total + (flux_z - pltpu.roll(flux_z, 1, 1))
        fz_ref[j] = fz
        residual_ref[j] = total
        done.append(total)
        if len(done) == group:
            forward_modes(
                j + 1 - group, done, scal[19], z_mat, y_mat, decay_ref, sweep_ref, ahead_ref, back_ref, corner_ref, power
            )
            done = []
    flux_low[...] = flux_x_low


def image_kernel(
    group, planes,
    scal, field_ref, field_next, fx_ref, fy_ref, fz_ref, fx_low, fy_low,
    x_jump, y_jump, z_mat, y_mat, decay_ref,
    image_ref, sweep_ref, ahead_ref, back_ref, corner_ref, sums_ref,
    flux_low, power,
):
    step = pl.program_id(0)
    rows, depth = flux_low.shape
    row = lax.broadcasted_iota(jnp.int32, (rows, depth), 0)

    @pl.when(step == 0)
    def _():
        flux_low[...] = fx_low[...] * x_jump[0]
        ahead_ref[...] = jnp.zeros_like(ahead_ref)
        back_ref[...] = jnp.zeros_like(back_ref)
        corner_ref[...] = jnp.zeros_like(corner_ref)
        power[...] = jnp.ones_like(power)
        sums_ref[...] = jnp.zeros_like(sums_ref)

    last = step == pl.num_programs(0) - 1
    end_jump = jnp.where(last, x_jump[1], field_next[0] - field_ref[planes - 1])
    flux_x_low = flux_low[...]
    sums = sums_ref[...]
    done = []
    for j in range(planes):
        x = step * planes + j
        field = field_ref[j]
        flux_x = fx_ref[j] * (field_ref[j + 1] - field if j + 1 < planes else end_jump)
        total = flux_x_low - flux_x
        flux_x_low = flux_x
        jump = jnp.where(row == rows - 1, y_jump[1, pl.ds(x, 1), :], pltpu.roll(field, rows - 1, 0) - field)
        flux_y = fy_ref[j] * jump
        low = fy_low[pl.ds(x, 1), :] * y_jump[0, pl.ds(x, 1), :]
        total = total + (jnp.where(row == 0, low, pltpu.roll(flux_y, 1, 0)) - flux_y)
        flux_z = fz_ref[j] * (pltpu.roll(field, depth - 1, 1) - field)
        total = total + (pltpu.roll(flux_z, 1, 1) - flux_z)
        image_ref[j] = total
        sums = sums + fold(field * total)
        done.append(total)
        if len(done) == group:
            forward_modes(
                j + 1 - group, done, scal[19], z_mat, y_mat, decay_ref, sweep_ref, ahead_ref, back_ref, corner_ref, power
            )
            done = []
    sums_ref[...] = sums
    flux_low[...] = flux_x_low


def local_kernel(
    devices, planes, summed,
    sweep_ref, ahead_ref, back_ref, corner_ref, decay_ref, border_ref, decay_inverse, decay_rest, *rest,
):
    if summed:
        sums_ref, earlier_ref, share_ref = rest[:3]
    out_ref, facts_ref, run, dots, rows_ref = rest[-5:]
    step = pl.program_id(0)
    blocks = pl.num_programs(0)
    decay = decay_ref[...]
    border = border_ref[...]
    half = decay.shape[0] // 2

    @pl.when(step == 0)
    def _():
        run[...] = ahead_ref[...] * decay_rest[...]
        dots[...] = jnp.zeros_like(dots)

    value, total = run[...], dots[...]
    first = (blocks - 1 - step) * planes
    for j in reversed(range(planes)):
        swept = sweep_ref[j]
        total = total + swept * swept
        value = swept + decay * value
        mode = value * border
        rows_ref[0, pl.ds(first + j, 1), :] = jnp.sum(mode[:half], axis=0, keepdims=True)
        rows_ref[1, pl.ds(first + j, 1), :] = jnp.sum(mode[half:], axis=0, keepdims=True)
    run[...] = value
    dots[...] = total

    @pl.when(step == blocks - 1)
    def _():
        part, width = out_ref.shape[2:]
        ahead = ahead_ref[...]
        ends = jnp.concatenate([ahead, back_ref[...]], axis=0)
        for slot, turned in enumerate((rows_ref[0].T, rows_ref[1].T, ends.T)):
            for j in range(devices):
                out_ref[j, slot] = turned[j * part : (j + 1) * part]
        lane = lax.broadcasted_iota(jnp.int32, facts_ref.shape, 1)
        square = jnp.sum(total * decay_inverse[...] + ahead * ahead * decay_rest[...])
        facts = jnp.where(lane == 0, square, 0.0) + jnp.where(lane == 1, jnp.sum(corner_ref[:1, :1]), 0.0)
        if summed:
            facts = facts + jnp.where(lane == 4, jnp.sum(sums_ref[...]), 0.0)
            facts = facts + pltpu.roll(earlier_ref[...] + share_ref[...], 2, 1)
        facts_ref[...] = facts


def faces_kernel(
    wide, narrow, part, sines, summed,
    device, got_ref, table_ref, capacity_ref, power_ref, mix_ref, row_even, row_odd, end_even, end_odd, row_dot,
    *rest,
):
    if summed:
        facts_ref, out_ref, jumps, modes = rest
    else:
        out_ref, share_ref, jumps, modes = rest
    devices = wide * narrow
    width = got_ref.shape[1]
    slots = 3
    out_slots = 4 if summed else 3
    faces = narrow - 1
    highest = dict(preferred_element_type=F32, precision=lax.Precision.HIGHEST)

    def take(ref, slot, mode, count):
        return ref[pl.ds(slot * part + mode, devices, stride=count * part), :]

    def incoming(ends, mode):
        swapped = pltpu.roll(ends, width // 2, 1)
        result = []
        for mine in range(wide):
            total = None
            for block in range(wide):
                at = slice(block * narrow, (block + 1) * narrow)
                term = mix_ref[0, mine, block, 0, pl.ds(mode, 1), :] * ends[at]
                term = term + mix_ref[0, mine, block, 1, pl.ds(mode, 1), :] * swapped[at]
                total = term if total is None else total + term
            result.append(total)
        return jnp.concatenate(result, axis=0)

    inner = None
    for mode in range(part):
        ends = take(got_ref, 2, mode, slots)
        entering = incoming(ends, mode)
        term = entering * pltpu.roll(ends, width // 2, 1) * row_dot[0, pl.ds(mode, 1), :]
        inner = term if inner is None else inner + term
        both = jnp.concatenate(
            [entering * row_even[0, pl.ds(mode, 1), :], entering * row_odd[0, pl.ds(mode, 1), :]], axis=0
        )
        added = jnp.dot(both, power_ref[mode], **highest)
        even = take(got_ref, 0, mode, slots) + added[:devices]
        odd = take(got_ref, 1, mode, slots) + added[devices:]
        jump = pltpu.roll(even + odd, devices - 1, 0) - (even - odd)
        jumps[pl.ds(mode, devices, stride=part), :] = jump
    mixed = None
    for block in range(wide):
        strips = [jumps[pl.ds((block * narrow + i) * part, part), :] for i in range(faces)]
        for k in range(faces):
            acc = None
            for i in range(faces):
                term = strips[i] * float(sines[k, i])
                acc = term if acc is None else acc + term
            modes[pl.ds(k * part, part), :] = acc
        term = jnp.dot(modes[...], table_ref[block], **highest)
        mixed = term if mixed is None else mixed + term
    plain = mixed
    mixed = mixed * capacity_ref[0]
    for block in range(wide):
        modes[...] = lax.dot_general(mixed, table_ref[block], (((1,), (1,)), ((), ())), **highest)
        solved = []
        for k in range(faces):
            acc = None
            for i in range(faces):
                term = modes[pl.ds(i * part, part), :] * float(sines[k, i])
                acc = term if acc is None else acc + term
            solved.append(acc)
        for strip in range(narrow):
            below = solved[strip - 1] if strip > 0 else jnp.zeros_like(solved[0])
            above = solved[strip] if strip < faces else jnp.zeros_like(solved[0])
            at = (block * narrow + strip) * out_slots * part
            out_ref[pl.ds(at, part), :] = above - below
            out_ref[pl.ds(at + part, part), :] = -(above + below)
    for mode in range(part):
        both = jnp.concatenate([take(out_ref, 0, mode, out_slots), take(out_ref, 1, mode, out_slots)], axis=0)
        added = lax.dot_general(both, power_ref[mode], (((1,), (1,)), ((), ())), **highest)
        added = pltpu.roll(added, width // 2, 1)
        ends = take(got_ref, 2, mode, slots) + end_even[0, pl.ds(mode, 1), :] * added[:devices]
        ends = ends + end_odd[0, pl.ds(mode, 1), :] * added[devices:]
        out_ref[pl.ds(2 * part + mode, devices, stride=out_slots * part), :] = incoming(ends, mode)
    share = jnp.sum(inner) - jnp.sum(plain * mixed)
    if summed:
        lane = lax.broadcasted_iota(jnp.int32, (part, width), 1)
        facts = facts_ref[:1, :width] + jnp.where(lane == 0, share, 0.0)
        for j in range(devices):
            out_ref[pl.ds((j * out_slots + 3) * part, part), :] = facts
    else:
        lane = lax.broadcasted_iota(jnp.int32, share_ref.shape, 1)
        share_ref[...] = jnp.where(lane == 0, share, 0.0)


def inverse_kernel(
    group, planes, dotted, voxels, mean_scale, shift,
    scal, faces_ref, sweep_ref, decay_ref, scale_ref, rest_inverse, decay_rest, rest_ref, y_mat, z_mat, *rest,
):
    if dotted:
        residual_ref, image_ref, along_ref, start_ref = rest[:4]
        out_ref, solution_ref, next_ref = rest[4:7]
    else:
        out_ref, jump_x, jump_y = rest[:3]
    run, added, rows_ref, entering, turned, factors = rest[-6:]
    terms = SHORT_TERMS if dotted else FULL_TERMS
    step = pl.program_id(0)
    blocks = pl.num_programs(0)
    decay = decay_ref[...]
    rows, depth = decay.shape
    half = rows // 2

    @pl.when(step == 0)
    def _():
        devices, _, part, _ = faces_ref.shape
        for slot in range(3):
            for j in range(devices):
                turned[pl.ds(j * part, part), :] = faces_ref[j, slot]
            if slot < 2:
                rows_ref[slot] = turned[...].T
            else:
                entering[...] = turned[...].T
        scale = scale_ref[...]

        def body(x, value):
            face = jnp.concatenate(
                [
                    jnp.broadcast_to(rows_ref[0, pl.ds(x, 1), :], (half, depth)),
                    jnp.broadcast_to(rows_ref[1, pl.ds(x, 1), :], (half, depth)),
                ],
                axis=0,
            )
            value = decay * value + scale * face
            added[x] = value
            return value

        value = lax.fori_loop(0, blocks * planes, body, entering[pl.ds(0, rows), :], unroll=8)
        value = value + sweep_ref[planes - 1]
        beyond = decay_rest[...] * value + rest_inverse[...] * entering[pl.ds(rows, rows), :]
        run[...] = beyond
        if not dotted:
            entering[pl.ds(rows, rows), :] = rest_ref[...] * beyond - value

        if dotted:
            total = faces_ref[0, 3]
            for j in range(1, devices):
                total = total + faces_ref[j, 3]
            total = total[:1]
            lane = lax.broadcasted_iota(jnp.int32, total.shape, 1)
            pick = lambda i: jnp.sum(jnp.where(lane == i, total, 0.0), axis=1, keepdims=True)
            base = scal[20]

            def solved(square, constant):
                mean = constant * (mean_scale / voxels)
                field = constant * base * (mean_scale * shift)
                return mean, field, base * square - mean * field

            mean, image_sum, square = solved(pick(0), pick(1))
            mean_along, _, rz_now = solved(pick(2), pick(3))
            alpha = rz_now / (pick(4) - mean_along * image_sum)
            ratio = alpha * (alpha * square) / rz_now
            for i, factor in enumerate((alpha, mean_along, ratio, ratio * mean_along - alpha * mean)):
                factors[pl.ds(i, 1), :] = jnp.broadcast_to(factor, (1, depth))

    value = run[...]
    first = (blocks - 1 - step) * planes
    if dotted:
        alpha, mean, ratio, offset = [
            jnp.broadcast_to(factors[pl.ds(i, 1), :], (rows, depth)) for i in range(4)
        ]
    for start in reversed(range(0, planes, group)):
        modes = [None] * group
        for j in reversed(range(group)):
            value = (sweep_ref[start + j] + added[first + start + j]) + decay * value
            modes[j] = value
        flat = jnp.concatenate(modes, axis=0)
        flat = product_left(y_mat, flat, terms)
        flat = product_right(flat, z_mat, terms)
        for j in range(group):
            at = start + j
            plane = flat[j * rows : (j + 1) * rows]
            if dotted:
                along = along_ref[at]
                next_ref[at] = residual_ref[at] - alpha * image_ref[at]
                solution_ref[at] = start_ref[at] + alpha * (along - mean)
                plane = (ratio * along - offset) - alpha * plane
            out_ref[at] = plane
    run[...] = value

    if not dotted:
        @pl.when(step == blocks - 1)
        def _():
            before = rest_ref[...] * run[...] - entering[pl.ds(0, rows), :]
            flat = jnp.concatenate([before, entering[pl.ds(rows, rows), :]] * (group // 2), axis=0)
            flat = product_left(y_mat, flat, terms)
            flat = product_right(flat, z_mat, terms)
            jump_x[0] = flat[:rows]
            jump_x[1] = flat[rows : 2 * rows]
            jump_y[0] = product_right(-0.5 * (rows_ref[0] + rows_ref[1]), z_mat, terms)
            jump_y[1] = product_right(0.5 * (rows_ref[0] - rows_ref[1]), z_mat, terms)


def whole(shape, single=False):
    mode = dict(pipeline_mode=pl.Buffered(1)) if single else {}
    return pl.BlockSpec(shape, lambda *_: (0,) * len(shape), **mode)


def shape_of(*dims):
    return jax.ShapeDtypeStruct(dims, F32)


def params(dims):
    return pltpu.CompilerParams(dimension_semantics=("arbitrary",) * dims, vmem_limit_bytes=VMEM_LIMIT)


def neighbours(axis):
    devices = lax.axis_size(axis)
    up = [(i, i + 1) for i in range(devices - 1)]
    return up, [(j, i) for i, j in up]


def exchange(first, last, axis):
    up, down = neighbours(axis)
    return lax.ppermute(last, axis, up), lax.ppermute(first, axis, down)


def solve(forward, tab, device, scal, earlier=(), final=()):
    sweep, ahead, back, corner = forward
    size_x, size_y, size_z = sweep.shape
    wide, narrow = lax.axis_size("wide"), lax.axis_size("narrow")
    devices = wide * narrow
    group, planes = tab["group"], tab["planes"]
    blocks = size_x // planes
    part = size_z // devices
    plane = (size_y, size_z)
    block = (planes,) + plane
    summed = bool(final)
    field = shape_of(size_x, *plane)
    long = min(2 * planes, size_x)
    behind = pl.BlockSpec(block, lambda i: (blocks - 1 - i, 0, 0))
    packed = (devices, 3, part, size_x)
    sent, facts = pl.pallas_call(
        functools.partial(local_kernel, devices, long, summed),
        grid=(size_x // long,),
        out_shape=(shape_of(*packed), shape_of(8, 128)),
        in_specs=[pl.BlockSpec((long,) + plane, lambda i: (size_x // long - 1 - i, 0, 0))]
        + [whole(plane)] * 2
        + [whole((8, 128))]
        + [whole(plane)] * 4
        + [whole((8, size_z)), whole((8, 128)), whole((8, 128))] * summed,
        out_specs=(whole(packed), whole((8, 128))),
        scratch_shapes=[pltpu.VMEM(plane, F32), pltpu.VMEM(plane, F32), pltpu.VMEM((2, size_x, size_z), F32)],
        compiler_params=params(1),
        name="strip_borders",
    )(
        sweep, ahead, back, corner, tab["decay"], tab["border"], tab["decay_inverse"], tab["decay_rest"],
        *earlier,
    )
    got = lax.all_to_all(sent, ("wide", "narrow"), split_axis=0, concat_axis=0, tiled=True)
    faces = narrow - 1
    length_x = wide * size_x
    flat = (devices * 3 * part, size_x)
    out_slots = 4 if summed else 3
    flat_out = (devices * out_slots * part, size_x)
    small = (whole((8, 128)),)
    mine = lambda shape: pl.BlockSpec((1,) + shape, lambda i, idx: (idx[0],) + (0,) * len(shape))
    solved, *share = pl.pallas_call(
        functools.partial(faces_kernel, wide, narrow, part, tab["sines"], summed),
        out_shape=(shape_of(*flat_out),) + (shape_of(8, 128),) * (not summed),
        grid_spec=pltpu.PrefetchScalarGridSpec(
            num_scalar_prefetch=1,
            grid=(1,),
            in_specs=[
                whole(flat),
                whole((wide, size_x, length_x)),
                mine((faces * part, length_x)),
                whole((part, 2 * size_y, size_x)),
                mine((wide, wide, 2, part, size_x)),
            ]
            + [mine((part, size_x))] * 5
            + list(small) * summed,
            out_specs=(whole(flat_out),) + small * (not summed),
            scratch_shapes=[
                pltpu.VMEM((devices * part, size_x), F32),
                pltpu.VMEM((faces * part, size_x), F32),
            ],
        ),
        compiler_params=params(1),
        name="strip_faces",
    )(
        device, got.reshape(flat), tab["table_x"], tab["capacity"], tab["decay_powers"], tab["mix"],
        tab["row_even"], tab["row_odd"], tab["end_even"], tab["end_odd"], tab["row_dot"],
        *([facts] if summed else []),
    )
    mine_now = lax.all_to_all(
        solved.reshape(devices, out_slots, part, size_x), ("wide", "narrow"), split_axis=0, concat_axis=0, tiled=True
    )
    operands = [
        scal, mine_now, sweep, tab["decay"], tab["border_decay"], tab["rest_inverse"], tab["decay_rest"],
        tab["rest"], tab["y_inv"], tab["z_inv"],
    ]
    smem = pl.BlockSpec(memory_space=pltpu.SMEM)
    in_specs = [smem, whole(mine_now.shape), behind] + [whole(plane)] * 5
    in_specs += [whole(tab["y_inv"].shape), whole(tab["z_inv"].shape)]
    if summed:
        operands += final
        in_specs += [behind] * 4
        out_shape = (field,) * 3
        out_specs = (behind,) * 3
    else:
        jumps = (2, size_x, size_z)
        out_shape = (field, shape_of(2, *plane), shape_of(*jumps))
        out_specs = (behind, whole((2,) + plane), whole(jumps))
    voxels = float(devices * size_x * size_y * size_z)
    result = pl.pallas_call(
        functools.partial(inverse_kernel, group, planes, summed, voxels, tab["mean_scale"], tab["shift"]),
        grid=(blocks,),
        out_shape=out_shape,
        in_specs=in_specs,
        out_specs=out_specs,
        scratch_shapes=[
            pltpu.VMEM(plane, F32),
            pltpu.VMEM((size_x,) + plane, F32),
            pltpu.VMEM((2, size_x, size_z), F32),
            pltpu.VMEM((2 * size_y, size_z), F32),
            pltpu.VMEM((size_z, size_x), F32),
            pltpu.VMEM((8, size_z), F32),
        ],
        compiler_params=params(1),
        name="inverse_modes",
    )(*operands)
    return result, [facts, *share]


def on_device(phase_ids, conduct_table, gradient, start_field):
    size_x, size_y, size_z = start_field.shape
    wide, narrow = lax.axis_size("wide"), lax.axis_size("narrow")
    tab = make_tables(size_x, size_y, size_z, wide, narrow)
    tab = {k: jnp.asarray(v) if isinstance(v, np.ndarray) and k != "sines" else v for k, v in tab.items()}
    group, planes = tab["group"], tab["planes"]
    blocks = size_x // planes
    plane = (size_y, size_z)
    block = (planes,) + plane
    wide_at, narrow_at = lax.axis_index("wide"), lax.axis_index("narrow")
    device = (wide_at * narrow + narrow_at).astype(jnp.int32)
    theta = lax.dynamic_index_in_dim(tab["theta"], device, 0, False)[:, :, None]
    along_x = jnp.arange(size_x, dtype=F32)
    tab["decay_powers"] = jnp.concatenate(
        [jnp.exp(-theta * along_x), jnp.exp(-theta * (size_x - 1.0 - along_x))], axis=1
    )
    device = device.reshape(1)
    flags = jnp.stack([wide_at > 0, wide_at < wide - 1, narrow_at > 0, narrow_at < narrow - 1])
    base = jnp.mean(conduct_table).reshape(1)
    scal = jnp.concatenate([(0.5 / conduct_table).T.reshape(-1), gradient, flags.astype(F32), 1.0 / base, base])
    scal, tab["decay_powers"], device = lax.optimization_barrier((scal, tab["decay_powers"], device))

    edge = lambda dim, at: jnp.stack(
        [lax.index_in_dim(phase_ids, at, dim, False).astype(F32), lax.index_in_dim(start_field, at, dim, False)]
    )
    x_before, x_after = exchange(edge(0, 0), edge(0, size_x - 1), "wide")
    y_before, y_after = exchange(edge(1, 0), edge(1, size_y - 1), "narrow")

    main = pl.BlockSpec(block, lambda i: (i, 0, 0))
    following = pl.BlockSpec((1,) + plane, lambda i: (jnp.minimum((i + 1) * planes, size_x - 1), 0, 0))
    field_shape = shape_of(size_x, *plane)
    end_shapes = (shape_of(*plane),) * 2 + (shape_of(8, 128),)
    end_specs = (whole(plane),) * 2 + (whole((8, 128)),)
    matrices = [whole(tab["z_fwd"].shape), whole(tab["y_fwd"].shape), whole(plane)]
    carried = [pltpu.VMEM(plane, F32), pltpu.VMEM(plane, F32)]
    residual, sweep, fx, fy, fz, fx_low, fy_low, *ends = pl.pallas_call(
        functools.partial(residual_kernel, group, planes),
        grid=(blocks,),
        out_shape=(field_shape,) * 5 + (shape_of(*plane), shape_of(size_x, size_z)) + end_shapes,
        in_specs=[pl.BlockSpec(memory_space=pltpu.SMEM), main, following, main, following]
        + [whole((2,) + plane)] * 2
        + [whole((2, size_x, size_z))] * 2
        + matrices,
        out_specs=(main,) * 5 + (whole(plane), whole((size_x, size_z))) + end_specs,
        scratch_shapes=carried,
        compiler_params=params(1),
        name="residual_modes",
    )(
        scal, phase_ids, phase_ids, start_field, start_field, x_before, x_after, y_before, y_after,
        tab["z_fwd"], tab["y_fwd"], tab["decay"],
    )
    (along, jump_x, jump_y), earlier = solve((sweep, *ends), tab, device, scal)

    image, sweep, *ends, sums = pl.pallas_call(
        functools.partial(image_kernel, group, planes),
        grid=(blocks,),
        out_shape=(field_shape,) * 2 + end_shapes + (shape_of(8, size_z),),
        in_specs=[pl.BlockSpec(memory_space=pltpu.SMEM), main, following] + [main] * 3
        + [whole(plane), whole((size_x, size_z))]
        + [whole((2,) + plane), whole((2, size_x, size_z))]
        + matrices,
        out_specs=(main,) * 2 + end_specs + (whole((8, size_z)),),
        scratch_shapes=carried,
        compiler_params=params(1),
        name="image_modes",
    )(
        scal, along, along, fx, fy, fz, fx_low, fy_low, jump_x, jump_y,
        tab["z_fwd"], tab["y_fwd"], tab["decay"],
    )
    (new_direction, result, residual_next), _ = solve(
        (sweep, *ends), tab, device, scal, [sums, *earlier], [residual, image, along, start_field]
    )
    return result, residual_next, new_direction


def solution(mesh):
    placed = (P("wide", "narrow", None), P(), P(), P("wide", "narrow", None))
    return jax.shard_map(
        on_device,
        mesh=mesh,
        in_specs=placed,
        out_specs=(P("wide", "narrow", None),) * 3,
        check_vma=False,
    )
```
